128 devices in a mesh: chan: 32 (over z_lo, y, x), seg: 4 (over z_hi, core).
Axes of the slice: x: 4, y: 4, z: 4 (z_hi: 2, z_lo: 2; z = z_hi * 2 + z_lo), core: 2. Of those that a mesh axis runs over, the one named last changes fastest.
Arguments:
- traces: bfloat16 [4096, 8, 8192], P('chan', 'seg'), may hold values from -20 to 20
- pair_offsets: int32 [32, 16], replicated, may hold values from 1 to 31, as said below
- pair_counts: int32 [32], replicated, may hold values from 1 to 16, 64 in all
- pair_owner: int32 [64], replicated, may hold values from 0 to 63, each once
Outputs:
- correlations: float32 [128, 64, 128, 256], P('seg', 'chan')
The draws below stay inside these ranges and needn't reach their ends.
Inputs may be any that keep to these rules, and one draw needn't show every extreme that they name: `pair_offsets`: row a lists 16 distinct offsets; only its first pair_counts[a] entries name pairs. `pair_counts`: the counts sum to 64. `pair_owner`: every slot number appears once.
All inputs are finite; a program needn't handle non-finite values.
Results may differ from the reference program's by a relative error of at most 0.017.
Values may be sent and summed in bfloat16 or wider, within the bound.
No kernel may reach another device: no remote copies, remote signals or barrier semaphores. Data moves between devices by JAX's collectives and lax.ppermute only.
A program may use at most 128 MiB of HBM per device.

```python
import math
import jax
import jax.numpy as jnp
import numpy as np
from jax import lax

BLOCK = 128
SAMPLES = 8192
BAND_START = 32
FREQS = 512
HALF = 8
LAGS = 256
NBLK = 32
CHANNELS = 4096
SEGS = 8
SLOTS = 64
MAXOFF = 16


def draw_traces(key, part):
    gain_key, noise_key = jax.random.split(key, 2)
    gains = 10.0 ** jax.random.uniform(gain_key, (CHANNELS, 1, 1), jnp.float32, -2.5, 0.5)
    noise = jnp.clip(jax.random.normal(noise_key, (CHANNELS, SEGS, SAMPLES), jnp.float32), -6.0, 6.0)
    return (gains * noise).astype(jnp.bfloat16)


def draw_pair_offsets(key, part):
    row_keys = jax.random.split(key, NBLK)

    def one_row(row_key):
        return jax.random.permutation(row_key, NBLK - 1)[:MAXOFF] + 1
    return jax.vmap(one_row)(row_keys).astype(jnp.int32)


def split_up(number_of, total, most, slope):
    loads = [(1 << 20) // math.isqrt(grade ** slope) + 1 for grade in range(2, number_of + 1)]
    rest, holding = total - most - (number_of - 1), [1] * (number_of - 1)
    while rest > 0:
        movable = [i for i in range(number_of - 1) if holding[i] < most]
        pool, left = sum([loads[i] for i in movable]), rest
        for i in movable:
            addition = min(most - holding[i], max(1, left * loads[i] // pool), rest)
            holding[i] = holding[i] + addition
            rest = rest - addition
    return np.array([most] + holding)


def ragged(rng, count, total, bound, slope):
    if count == 2:
        one = jax.random.randint(rng, (), max(1, total - bound), min(bound, total - 1) + 1)
        return jnp.stack([one, total - one])
    sizes = jnp.asarray(split_up(count, total, bound, slope), jnp.int32)
    twos = (count - 1) // 2
    source_of, taker = sizes[1:1 + 2 * twos:2], sizes[2:2 + 2 * twos:2]
    room = jnp.minimum(source_of - 1, bound - taker)
    passed = jax.random.randint(jax.random.fold_in(rng, 1), (twos,), 0, 1 << 20) % (room + 1)
    sizes = sizes.at[1:1 + 2 * twos:2].set(source_of - passed).at[2:2 + 2 * twos:2].set(taker + passed)
    return sizes[jax.random.permutation(jax.random.fold_in(rng, 2), count)]


def setup_inputs(seed: int = 0) -> dict:
    streams_of = jax.random.split(jax.random.key(seed), 5)
    traces = draw_traces(jax.random.fold_in(streams_of[4], 71), 0)
    pair_offsets = draw_pair_offsets(jax.random.fold_in(streams_of[4], 71), 0)
    pair_counts = ragged(streams_of[2], NBLK, SLOTS, MAXOFF, 2).astype(jnp.int32)
    pair_owner = jax.random.permutation(streams_of[3], SLOTS).astype(jnp.int32)
    return {"traces": traces, "pair_offsets": pair_offsets, "pair_counts": pair_counts, "pair_owner": pair_owner}


def smoother(bin_count):
    bins_axis = lax.iota(jnp.int32, bin_count)
    nearby = (jnp.abs(bins_axis[:, None] - bins_axis[None, :]) <= HALF).astype(jnp.float32)
    return nearby / lax.optimization_barrier(jnp.sum(nearby, axis=0, keepdims=True))

def lag_table(first_bin, bin_count):
    bins_axis = BAND_START + first_bin + lax.iota(jnp.int32, bin_count)
    shifts = jnp.mod(lax.iota(jnp.int32, LAGS) - LAGS // 2, SAMPLES)
    phase_index = jnp.mod(bins_axis[:, None] * shifts[None, :], SAMPLES)
    angles = phase_index.astype(jnp.float32) * (2.0 * math.pi / SAMPLES)
    return jnp.concatenate([jnp.cos(angles), -jnp.sin(angles)], axis=0).astype(jnp.bfloat16)

def pair_blocks(pair_offsets, pair_counts, pair_owner, block_count, slot_count):
    slot_index = lax.iota(jnp.int32, slot_count)
    starts = (jnp.cumsum(pair_counts) - pair_counts).astype(jnp.int32)
    first_block = lax.optimization_barrier(jnp.sum((starts[None, :] <= slot_index[:, None]).astype(jnp.int32), axis=1)) - 1
    member = lax.iota(jnp.int32, block_count)[None, :] == first_block[:, None]
    start_of = lax.optimization_barrier(jnp.sum(jnp.where(member, starts[None, :], 0), axis=1))
    position = slot_index - start_of
    listed = lax.optimization_barrier(jnp.sum(jnp.where(member[:, :, None], pair_offsets[None, :, :], 0), axis=1))
    chosen = lax.iota(jnp.int32, pair_offsets.shape[1])[None, :] == position[:, None]
    offset = lax.optimization_barrier(jnp.sum(jnp.where(chosen, listed, 0), axis=1))
    second_block = jnp.mod(first_block + offset, block_count)
    held = pair_owner[None, :] == slot_index[:, None]
    slot_first = lax.optimization_barrier(jnp.sum(jnp.where(held, first_block[None, :], 0), axis=1)).astype(jnp.int32)
    slot_second = lax.optimization_barrier(jnp.sum(jnp.where(held, second_block[None, :], 0), axis=1)).astype(jnp.int32)
    return (slot_first, slot_second)

def whiten(block_traces):
    spectrum = jnp.fft.rfft(block_traces.astype(jnp.float32), axis=-1)[:, :, BAND_START:BAND_START + FREQS]
    real_part = jnp.real(spectrum)
    imag_part = jnp.imag(spectrum)
    amplitude = jnp.sqrt(real_part * real_part + imag_part * imag_part)
    smoothed = jnp.dot(amplitude.reshape(-1, FREQS), smoother(FREQS), precision=lax.Precision.HIGHEST).reshape(amplitude.shape)
    divisor = jnp.maximum(smoothed, 1.0)
    return jnp.stack([real_part / divisor, imag_part / divisor], axis=2).astype(jnp.bfloat16)

def reference(traces, pair_offsets, pair_counts, pair_owner):
    whitened = lax.map(whiten, traces.reshape(NBLK, BLOCK, SEGS, SAMPLES))
    slot_first, slot_second = pair_blocks(pair_offsets, pair_counts, pair_owner, NBLK, SLOTS)
    table = lag_table(0, FREQS)
    norm_factor = 1.0 / math.sqrt(FREQS * SEGS)

    def one_slot(blocks):
        first_spec = whitened[blocks[0]].astype(jnp.float32)
        second_spec = whitened[blocks[1]].astype(jnp.float32)
        turned = jnp.stack([first_spec[:, :, 1], -first_spec[:, :, 0]], axis=2)
        real_part = jnp.einsum('ispf,jspf->ijf', first_spec, second_spec, precision=lax.Precision.HIGHEST)
        imag_part = jnp.einsum('ispf,jspf->ijf', turned, second_spec, precision=lax.Precision.HIGHEST)
        cross = jnp.stack([real_part, imag_part], axis=2).astype(jnp.bfloat16)
        lagged = jnp.dot(cross.reshape(-1, 2 * FREQS), table, preferred_element_type=jnp.float32) * norm_factor
        return lagged.reshape(BLOCK, BLOCK, LAGS)
    stacked = lax.map(one_slot, jnp.stack([slot_first, slot_second], axis=1))
    return jnp.transpose(stacked, (1, 0, 2, 3))
```

```python
import math

import jax
import jax.numpy as jnp
import ml_dtypes
import numpy as np
from jax import lax
from jax.experimental import pallas as pl
from jax.experimental.pallas import tpu as pltpu
from jax.sharding import PartitionSpec as P

SAMPLES = 8192
BAND_START = 32
FREQS = 512
HALF = 8
LAGS = 256
BLOCK = 128
NBLK = 32
SEGS = 8
SLOT_DEV = 2
GROUP = 16
VMEM = 56 * 1024 * 1024


def dft_tables():
    phase = np.outer(np.arange(SAMPLES), BAND_START + np.arange(FREQS)) % SAMPLES
    ring = 2.0 * math.pi / SAMPLES * np.arange(SAMPLES)
    table = np.concatenate([np.cos(ring)[phase], -np.sin(ring)[phase]], axis=1)
    high = table.astype(np.float32).astype(ml_dtypes.bfloat16)
    low = (table - high.astype(np.float64)).astype(np.float32).astype(ml_dtypes.bfloat16)
    return high, low


def band_matrix():
    bins = np.arange(FREQS)
    near = np.abs(bins[:, None] - bins[None, :]) <= HALF
    return near.astype(ml_dtypes.bfloat16), near.sum(axis=0, keepdims=True).astype(np.float32)


def lag_tables():
    shifts = (np.arange(LAGS) - LAGS // 2) % SAMPLES
    phase = np.outer(BAND_START + np.arange(FREQS), shifts) % SAMPLES
    angles = phase.astype(np.float32) * np.float32(2.0 * math.pi / SAMPLES)
    norm = 1.0 / math.sqrt(FREQS * SEGS)
    parts = np.stack([np.cos(angles), -np.sin(angles)]).astype(ml_dtypes.bfloat16)
    parts = (parts.astype(np.float32) * norm).astype(ml_dtypes.bfloat16)
    parts = parts.reshape(2, FREQS // GROUP, 2, GROUP // 2, LAGS).transpose(4, 1, 0, 2, 3)
    both = np.stack([parts, parts[:, :, :, ::-1]])
    return both.reshape(2, LAGS, 2 * FREQS)


def group_mask():
    lane = np.arange(256)
    own = (lane // 16 % 2) * 8 + lane % 8
    return (np.arange(GROUP)[:, None] == own[None, :]).astype(np.float32)


def pair_blocks(pair_offsets, pair_counts, pair_owner, block_count, slot_count):
    slot_index = lax.iota(jnp.int32, slot_count)
    starts = jnp.cumsum(pair_counts) - pair_counts
    first_block = jnp.sum((starts[None, :] <= slot_index[:, None]).astype(jnp.int32), axis=1) - 1
    member = lax.iota(jnp.int32, block_count)[None, :] == first_block[:, None]
    start_of = jnp.sum(jnp.where(member, starts[None, :], 0), axis=1)
    position = slot_index - start_of
    listed = jnp.sum(jnp.where(member[:, :, None], pair_offsets[None, :, :], 0), axis=1)
    chosen = lax.iota(jnp.int32, pair_offsets.shape[1])[None, :] == position[:, None]
    offset = jnp.sum(jnp.where(chosen, listed, 0), axis=1)
    second_block = jnp.mod(first_block + offset, block_count)
    held = pair_owner[None, :] == slot_index[:, None]
    slot_first = jnp.sum(jnp.where(held, first_block[None, :], 0), axis=1)
    slot_second = jnp.sum(jnp.where(held, second_block[None, :], 0), axis=1)
    return (slot_first, slot_second)


def whiten_kernel(spec_ref, band_ref, count_ref, out_ref, tile_ref):
    band = band_ref[...]
    for tile in range(8):
        tile_ref[tile] = spec_ref[:, tile * BLOCK : (tile + 1) * BLOCK]
    turned = []
    for seg in range(2):
        rows = pl.ds(seg, BLOCK, stride=2)
        real = jnp.concatenate([tile_ref[tile, rows, :] for tile in range(4)], axis=1)
        imag = jnp.concatenate([tile_ref[tile, rows, :] for tile in range(4, 8)], axis=1)
        amplitude = jnp.sqrt(real * real + imag * imag)
        high = amplitude.astype(jnp.bfloat16)
        low = (amplitude - high.astype(jnp.float32)).astype(jnp.bfloat16)
        total = jnp.dot(high, band, preferred_element_type=jnp.float32)
        total = total + jnp.dot(low, band, preferred_element_type=jnp.float32)
        divisor = jnp.maximum(total / count_ref[...], 1.0)
        turned.append([(real / divisor).T, (imag / divisor).T])
    for part in range(2):
        pieces = [turned[seg][part].reshape(FREQS // 8, 1, 8, BLOCK) for seg in range(2)]
        both = jnp.concatenate(pieces, axis=1).reshape(NBLK, 2 * GROUP, BLOCK)
        out_ref[:, part * 2 * GROUP : (part + 1) * 2 * GROUP, :] = both.astype(jnp.bfloat16)


def select_kernel(first_ref, second_ref, place_ref, held_ref, out_ref, rows_ref):
    lane = lax.broadcasted_iota(jnp.int32, (32, BLOCK), 1)
    left = (lane < 64) == (place_ref[0] % 2 == 0)

    def turn(block, carry):
        tiles = held_ref[block].astype(jnp.float32)
        for core in range(2):
            order = tiles if core == 0 else jnp.concatenate(
                [tiles[16:32], tiles[0:16], tiles[48:64], tiles[32:48]], axis=0
            )
            twice = jnp.concatenate([order, order], axis=0)
            rows_ref[core, block] = twice.T.astype(jnp.bfloat16)
        return carry

    lax.fori_loop(0, NBLK, turn, 0)

    def send(chan, carry):
        slots = [SLOT_DEV * chan + slot for slot in range(SLOT_DEV)]
        for seg in range(4):
            core = seg % 2
            dest = 4 * chan + seg
            for slot in range(SLOT_DEV):
                second = second_ref[slots[slot]]
                for part in range(2):
                    out_ref[dest, pl.ds(32 * slot + 16 * part, 16), :] = held_ref[
                        second, pl.ds(32 * part + 16 * core, 16), :
                    ]
            one = rows_ref[core, first_ref[slots[0]], pl.ds(32 * seg, 32), :]
            two = rows_ref[core, first_ref[slots[1]], pl.ds(32 * seg, 32), :]
            out_ref[dest, pl.ds(64, 32), :] = jnp.where(left, one, two)
        return carry

    lax.fori_loop(0, NBLK, send, 0)


def correlate_kernel(core_ref, own_ref, other_ref, mask_ref, table_ref, out_ref, cross_ref):
    slot = pl.program_id(0)
    lane = lax.broadcasted_iota(jnp.int32, (32, BLOCK), 1)
    left = (lane < 64) == (slot == 0)

    def cross(group, carry):
        order = [slot, 1 - slot, 2 + slot, 3 - slot]
        upper = []
        lower = []
        for seg in order:
            src = 4 * group + seg
            tiles = []
            for part in range(2):
                rows = pl.ds(pl.multiple_of(32 * slot + 16 * part, 16), 16)
                tiles.append([own_ref[src, rows, :], other_ref[src, rows, :]])
            upper += tiles[0] + tiles[1]
            lower += [-tiles[1][0], -tiles[1][1], tiles[0][0], tiles[0][1]]
        second = jnp.concatenate(
            [jnp.concatenate(upper, axis=0), jnp.concatenate(lower, axis=0)], axis=1
        )
        lanes = [own_ref[4 * group + seg, pl.ds(64, 32), :] for seg in range(4)]
        first = jnp.concatenate(
            [jnp.where(left, lanes[0], lanes[1]), jnp.where(left, lanes[2], lanes[3])], axis=1
        ).astype(jnp.float32)
        mask = mask_ref[...]
        spread = [
            (jnp.broadcast_to(first[i : i + 1], (GROUP, 256)) * mask).astype(jnp.bfloat16)
            for i in range(32)
        ]
        found = jnp.dot(
            jnp.concatenate(spread, axis=0), second, preferred_element_type=jnp.float32
        ).astype(jnp.bfloat16)
        for part in range(2):
            cross_ref[:, 2 * group + part] = found[:, part * BLOCK : (part + 1) * BLOCK].reshape(
                32, GROUP, BLOCK
            )
        return carry

    lax.fori_loop(0, NBLK, cross, 0)

    def lags(pair, carry):
        sides = [cross_ref[2 * pair + k].reshape(2 * FREQS, BLOCK) for k in range(2)]
        lagged = jnp.dot(
            table_ref[0], jnp.concatenate(sides, axis=1), preferred_element_type=jnp.float32
        )
        for k in range(2):
            out_ref[2 * pair + k, 0] = lagged[:, k * BLOCK : (k + 1) * BLOCK].T
        return carry

    lax.fori_loop(0, 16, lags, 0)


def whiten(spectrum):
    band, count = band_matrix()
    return pl.pallas_call(
        whiten_kernel,
        out_shape=jax.ShapeDtypeStruct((NBLK, 4 * GROUP, BLOCK), jnp.bfloat16),
        scratch_shapes=[pltpu.VMEM((8, 2 * BLOCK, BLOCK), jnp.float32)],
        compiler_params=pltpu.CompilerParams(vmem_limit_bytes=VMEM),
        name="whiten",
    )(spectrum, jnp.asarray(band), jnp.asarray(count))


def select(slot_first, slot_second, place, held):
    smem = pl.BlockSpec(memory_space=pltpu.SMEM)
    return pl.pallas_call(
        select_kernel,
        out_shape=jax.ShapeDtypeStruct((128, 96, BLOCK), jnp.bfloat16),
        in_specs=[smem, smem, smem, pl.BlockSpec(memory_space=pltpu.VMEM)],
        scratch_shapes=[pltpu.VMEM((2, NBLK, BLOCK, BLOCK), jnp.bfloat16)],
        compiler_params=pltpu.CompilerParams(vmem_limit_bytes=VMEM),
        name="select",
    )(slot_first, slot_second, place, held)


def correlate(core, own, other):
    whole = lambda *shape: pl.BlockSpec(
        shape, lambda s, c: (0,) * len(shape), pipeline_mode=pl.Buffered(1)
    )
    return pl.pallas_call(
        correlate_kernel,
        out_shape=jax.ShapeDtypeStruct((32, SLOT_DEV, BLOCK, LAGS), jnp.float32),
        grid_spec=pltpu.PrefetchScalarGridSpec(
            num_scalar_prefetch=1,
            grid=(SLOT_DEV,),
            in_specs=[
                whole(128, 96, BLOCK),
                whole(128, 64, BLOCK),
                whole(GROUP, 256),
                pl.BlockSpec((1, LAGS, 2 * FREQS), lambda s, c: (c[0], 0, 0)),
            ],
            out_specs=pl.BlockSpec((32, 1, BLOCK, LAGS), lambda s, c: (0, s, 0, 0)),
            scratch_shapes=[pltpu.VMEM((32, 2 * FREQS // GROUP, GROUP, BLOCK), jnp.bfloat16)],
        ),
        compiler_params=pltpu.CompilerParams(vmem_limit_bytes=VMEM),
        name="correlate",
    )(core, own, other, jnp.asarray(group_mask()), jnp.asarray(lag_tables()))


def on_device(traces, pair_offsets, pair_counts, pair_owner):
    signal = traces.reshape(2 * BLOCK, SAMPLES)
    high, low = dft_tables()
    spectrum = jnp.dot(signal, jnp.asarray(high), preferred_element_type=jnp.float32)
    spectrum = spectrum + jnp.dot(signal, jnp.asarray(low), preferred_element_type=jnp.float32)
    slot_first, slot_second = pair_blocks(
        pair_offsets, pair_counts, pair_owner, NBLK, SLOT_DEV * NBLK
    )
    seg = lax.axis_index("seg").astype(jnp.int32).reshape(1)
    held = lax.all_to_all(whiten(spectrum), "chan", split_axis=0, concat_axis=0, tiled=True)
    sent = select(slot_first, slot_second, seg, held)
    own = lax.all_to_all(sent, ("chan", "seg"), split_axis=0, concat_axis=0, tiled=True)
    other = lax.ppermute(own[:, :64], "seg", [(0, 1), (1, 0), (2, 3), (3, 2)])
    return correlate(seg % 2, own, other)


def solution(mesh):
    placed = (P("chan", "seg", None), P(), P(), P())
    return jax.shard_map(
        on_device,
        mesh=mesh,
        in_specs=placed,
        out_specs=P("seg", "chan", None, None),
        check_vma=False,
    )
```

```python
import math

import jax
import jax.numpy as jnp
import ml_dtypes
import numpy as np
from jax import lax
from jax.experimental import pallas as pl
from jax.experimental.pallas import tpu as pltpu
from jax.sharding import PartitionSpec as P

SAMPLES = 8192
BAND_START = 32
FREQS = 512
HALF = 8
LAGS = 256
BLOCK = 128
NBLK = 32
SEGS = 8
SLOT_DEV = 2
GROUP = 16
RADIX = 16
VMEM = 32 * 1024 * 1024
PAIRS = 4
UNROLL = 32
FETCHES = 8


def bin_order():
    residues = [(0, 8)] + [(unit, RADIX - unit) for unit in range(1, RADIX // 2)]
    return (np.array(residues)[:, :, None] + RADIX * np.arange(FREQS // RADIX)).reshape(-1)


def dft_tables():
    run = SAMPLES // RADIX
    ring = 2.0 * math.pi / SAMPLES * np.arange(SAMPLES)
    bins = bin_order().reshape(RADIX // 2, 2, FREQS // RADIX)
    table = np.zeros((RADIX // 2, 2, run, 2, 2, FREQS // RADIX))
    for unit in range(RADIX // 2):
        for side in range(2):
            phase = np.outer(np.arange(run), BAND_START + bins[unit, side]) % SAMPLES
            cosine, sine = np.cos(ring)[phase], np.sin(ring)[phase]
            if unit == 0:
                table[unit, side, :, 0, side] = cosine
                table[unit, side, :, 1, side] = -sine
            else:
                sign = 1.0 if side == 0 else -1.0
                table[unit, 0, :, 0, side] = cosine
                table[unit, 0, :, 1, side] = -sine
                table[unit, 1, :, 0, side] = -sign * sine
                table[unit, 1, :, 1, side] = -sign * cosine
    table = table.reshape(RADIX // 2, 2 * run, BLOCK)
    high = table.astype(np.float32).astype(ml_dtypes.bfloat16)
    low = (table - high.astype(np.float64)).astype(np.float32).astype(ml_dtypes.bfloat16)
    return np.concatenate([high, low], axis=2)


def band_tables():
    bins = bin_order()
    near = np.abs(bins[:, None] - bins[None, :]) <= HALF
    order = np.arange(FREQS)[:, None] == bins[None, :]
    return (
        near.astype(ml_dtypes.bfloat16),
        order.astype(ml_dtypes.bfloat16),
    )


def lag_tables():
    shifts = (np.arange(LAGS) - LAGS // 2) % SAMPLES
    phase = np.outer(BAND_START + np.arange(FREQS), shifts) % SAMPLES
    angles = phase.astype(np.float32) * np.float32(2.0 * math.pi / SAMPLES)
    norm = 1.0 / math.sqrt(FREQS * SEGS)
    parts = np.stack([np.cos(angles), -np.sin(angles)]).astype(ml_dtypes.bfloat16)
    parts = (parts.astype(np.float32) * norm).astype(ml_dtypes.bfloat16)
    parts = parts.reshape(2, FREQS // GROUP, 2, GROUP // 2, LAGS).transpose(4, 1, 0, 2, 3)
    both = np.stack([parts, parts[:, :, :, ::-1]])
    return both.reshape(2, LAGS, 2 * FREQS)


def group_mask():
    lane = np.arange(256)
    own = (lane // 16 % 2) * 8 + lane % 8
    return (np.arange(GROUP)[:, None] == own[None, :]).astype(ml_dtypes.bfloat16)


def pair_blocks(pair_offsets, pair_counts, pair_owner, block_count, slot_count):
    slot_index = lax.iota(jnp.int32, slot_count)
    starts = jnp.cumsum(pair_counts) - pair_counts
    first_block = jnp.sum((starts[None, :] <= slot_index[:, None]).astype(jnp.int32), axis=1) - 1
    member = lax.iota(jnp.int32, block_count)[None, :] == first_block[:, None]
    start_of = jnp.sum(jnp.where(member, starts[None, :], 0), axis=1)
    position = slot_index - start_of
    listed = jnp.sum(jnp.where(member[:, :, None], pair_offsets[None, :, :], 0), axis=1)
    chosen = lax.iota(jnp.int32, pair_offsets.shape[1])[None, :] == position[:, None]
    offset = jnp.sum(jnp.where(chosen, listed, 0), axis=1)
    second_block = jnp.mod(first_block + offset, block_count)
    held = pair_owner[None, :] == slot_index[:, None]
    slot_first = jnp.sum(jnp.where(held, first_block[None, :], 0), axis=1)
    slot_second = jnp.sum(jnp.where(held, second_block[None, :], 0), axis=1)
    return (slot_first, slot_second)


def butterflies(x):
    root, c1, c3 = math.sqrt(0.5), math.cos(math.pi / 8), math.cos(3 * math.pi / 8)
    a = [x[n] + x[n + 8] for n in range(8)]
    b = [x[n] - x[n + 8] for n in range(8)]
    c = [a[n] + a[n + 4] for n in range(4)]
    d = [a[n] - a[n + 4] for n in range(4)]
    even, odd = c[0] + c[2], c[1] + c[3]
    g, h = (d[1] - d[3]) * root, (d[1] + d[3]) * root
    p = [None] + [b[n] - b[8 - n] for n in range(1, 4)]
    q = [None] + [b[n] + b[8 - n] for n in range(1, 4)]
    p2, q2 = p[2] * root, q[2] * root
    re1, re3 = p[1] * c1 + p[3] * c3, p[1] * c3 - p[3] * c1
    im1, im3 = q[1] * c3 + q[3] * c1, q[1] * c1 - q[3] * c3
    plus, minus = b[0] + p2, b[0] - p2
    over, under = q2 + b[4], q2 - b[4]
    return [
        (even + odd, even - odd),
        (plus + re1, im1 + over),
        (d[0] + g, d[2] + h),
        (minus + re3, im3 + under),
        (c[0] - c[2], c[1] - c[3]),
        (minus - re3, im3 - under),
        (d[0] - g, h - d[2]),
        (plus - re1, im1 - over),
    ]


def front_kernel(
    rows_hbm, dft_hbm, band_hbm, order_hbm, out_ref,
    rows_ref, dft_ref, band_ref, order_ref, sums_ref, row_sem, table_sem,
):
    each = BLOCK * BLOCK // FETCHES
    copies = []
    for fetch in range(FETCHES):
        part = pl.ds(each * fetch, each)
        copies.append(
            pltpu.make_async_copy(rows_hbm.at[part], rows_ref.at[part], row_sem.at[fetch])
        )
        copies[fetch].start()
    fetched = [(dft_hbm, dft_ref), (band_hbm, band_ref), (order_hbm, order_ref)]
    tables = [
        pltpu.make_async_copy(source, target, table_sem.at[which])
        for which, (source, target) in enumerate(fetched)
    ]
    for table in tables:
        table.start()

    def channel(chan, carry):
        x = []
        for pair in range(RADIX // 2):
            tile = rows_ref[pl.ds(pl.multiple_of(BLOCK * chan + 16 * pair, 16), 16), :]
            tile = tile.astype(jnp.float32)
            x += [tile[:8], tile[8:]]
        for unit, sums in enumerate(butterflies(x)):
            for side in range(2):
                sums_ref[2 * unit + side, pl.ds(pl.multiple_of(8 * chan, 8), 8), :] = sums[side]
        return carry

    for fetch in range(FETCHES):
        copies[fetch].wait()
        count = BLOCK // FETCHES
        lax.fori_loop(count * fetch, count * (fetch + 1), channel, 0, unroll=4)

    for table in tables:
        table.wait()
    found = []
    for unit in range(RADIX // 2):
        columns = []
        for side in range(2):
            for tile in range(4):
                part = [
                    sums_ref[2 * unit + side, pl.ds(2 * tile + seg, BLOCK, stride=8), :]
                    for seg in range(2)
                ]
                columns.append(jnp.concatenate(part, axis=0))
        exact = jnp.concatenate(columns, axis=1)
        high = exact.astype(jnp.bfloat16)
        low = (exact - high.astype(jnp.float32)).astype(jnp.bfloat16)
        first = jnp.dot(high, dft_ref[unit], preferred_element_type=jnp.float32)
        rest = jnp.dot(low, dft_ref[unit, :, :BLOCK], preferred_element_type=jnp.float32)
        found.append(first[:, :BLOCK] + (first[:, BLOCK:] + rest))
    left = lax.broadcasted_iota(jnp.int32, (2 * BLOCK, BLOCK), 1) < 64
    real = []
    imag = []
    for one, two in zip(found[0::2], found[1::2]):
        real.append(jnp.where(left, one, pltpu.roll(two, 64, 1)))
        imag.append(jnp.where(left, pltpu.roll(one, 64, 1), two))
    real = jnp.concatenate(real, axis=1)
    imag = jnp.concatenate(imag, axis=1)
    amplitude = jnp.sqrt(real * real + imag * imag)
    high = amplitude.astype(jnp.bfloat16)
    low = (amplitude - high.astype(jnp.float32)).astype(jnp.bfloat16)
    band = band_ref[...]
    total = jnp.dot(high, band, preferred_element_type=jnp.float32)
    total = total + jnp.dot(low, band, preferred_element_type=jnp.float32)
    count = jnp.dot(jnp.ones((8, FREQS), jnp.bfloat16), band, preferred_element_type=jnp.float32)
    divisor = jnp.maximum(total / count[:1], 1.0)
    for part, spectrum in enumerate([real, imag]):
        white = (spectrum / divisor).astype(jnp.bfloat16)
        turned = lax.dot_general(
            order_ref[...], white, (((1,), (1,)), ((), ())), preferred_element_type=jnp.float32
        )
        pieces = [
            turned[:, BLOCK * seg : BLOCK * (seg + 1)].reshape(FREQS // 8, 1, 8, BLOCK)
            for seg in range(2)
        ]
        both = jnp.concatenate(pieces, axis=1).reshape(NBLK, 2 * GROUP, BLOCK)
        out_ref[:, part * 2 * GROUP : (part + 1) * 2 * GROUP, :] = both.astype(jnp.bfloat16)


def select_kernel(first_ref, second_ref, place_ref, held_ref, out_ref, rows_ref):
    lane = lax.broadcasted_iota(jnp.int32, (32, BLOCK), 1)
    left = (lane < 64) == (place_ref[0] % 2 == 0)

    def turn(block, carry):
        tiles = held_ref[block].astype(jnp.float32)
        for core in range(2):
            order = tiles if core == 0 else jnp.concatenate(
                [tiles[16:32], tiles[0:16], tiles[48:64], tiles[32:48]], axis=0
            )
            twice = jnp.concatenate([order, order], axis=0)
            rows_ref[core, block] = twice.T.astype(jnp.bfloat16)
        return carry

    lax.fori_loop(0, NBLK, turn, 0)

    def send(chan, carry):
        slots = [SLOT_DEV * chan + slot for slot in range(SLOT_DEV)]
        for seg in range(4):
            core = seg % 2
            dest = 4 * chan + seg
            for slot in range(SLOT_DEV):
                second = second_ref[slots[slot]]
                for part in range(2):
                    out_ref[dest, pl.ds(32 * slot + 16 * part, 16), :] = held_ref[
                        second, pl.ds(32 * part + 16 * core, 16), :
                    ]
            one = rows_ref[core, first_ref[slots[0]], pl.ds(32 * seg, 32), :]
            two = rows_ref[core, first_ref[slots[1]], pl.ds(32 * seg, 32), :]
            out_ref[dest, pl.ds(64, 32), :] = jnp.where(left, one, two)
        return carry

    lax.fori_loop(0, NBLK, send, 0)


def correlate_kernel(
    core_ref, own_ref, other_ref, mask_ref, table_ref, out_hbm, cross_ref, lag_ref, out_sem
):
    core = core_ref[0]
    leaving = []
    for slot in range(SLOT_DEV):

        def cross(group, carry):
            order = [slot, 1 - slot, 2 + slot, 3 - slot]
            upper = []
            lower = []
            for seg in order:
                src = 4 * group + seg
                tiles = []
                for part in range(2):
                    rows = pl.ds(32 * slot + 16 * part, 16)
                    tiles.append([own_ref[src, rows, :], other_ref[src, rows, :]])
                upper += tiles[0] + tiles[1]
                lower += [-tiles[1][0], -tiles[1][1]] + tiles[0]
            second = jnp.concatenate(
                [jnp.concatenate(upper, axis=0), jnp.concatenate(lower, axis=0)], axis=1
            )
            lane = lax.broadcasted_iota(jnp.int32, (32, BLOCK), 1)
            left = (lane < 64) == (slot == 0)
            lanes = [own_ref[4 * group + seg, pl.ds(64, 32), :] for seg in range(4)]
            first = jnp.concatenate(
                [jnp.where(left, lanes[0], lanes[1]), jnp.where(left, lanes[2], lanes[3])], axis=1
            )
            mask = mask_ref[...]
            spread = [jnp.broadcast_to(first[i : i + 1], (GROUP, 256)) * mask for i in range(32)]
            found = jnp.dot(
                jnp.concatenate(spread, axis=0), second, preferred_element_type=jnp.float32
            ).astype(jnp.bfloat16)
            for part in range(2):
                cross_ref[:, 2 * group + part] = found[
                    :, part * BLOCK : (part + 1) * BLOCK
                ].reshape(32, GROUP, BLOCK)
            return carry

        def lags(pair, carry):
            sides = [cross_ref[2 * pair + k].reshape(2 * FREQS, BLOCK) for k in range(2)]
            lagged = jnp.dot(
                table_ref[core], jnp.concatenate(sides, axis=1), preferred_element_type=jnp.float32
            )
            for k in range(2):
                lag_ref[slot, 2 * pair + k] = lagged[:, k * BLOCK : (k + 1) * BLOCK].T
            return carry

        lax.fori_loop(0, NBLK, cross, 0, unroll=UNROLL)
        for step in range(16 // PAIRS):
            lax.fori_loop(PAIRS * step, PAIRS * (step + 1), lags, 0, unroll=True)
            rows = pl.ds(2 * PAIRS * step, 2 * PAIRS)
            copy = pltpu.make_async_copy(
                lag_ref.at[slot, rows], out_hbm.at[rows, slot], out_sem.at[slot, step]
            )
            copy.start()
            leaving.append(copy)
    for copy in leaving:
        copy.wait()


def front(traces):
    band, order = band_tables()
    rows = traces.reshape(BLOCK, 2, SAMPLES // BLOCK, BLOCK).transpose(0, 2, 1, 3)
    rows = rows.reshape(BLOCK * BLOCK, BLOCK)
    vmem = pl.BlockSpec(memory_space=pltpu.VMEM)
    return pl.pallas_call(
        front_kernel,
        out_shape=jax.ShapeDtypeStruct((NBLK, 4 * GROUP, BLOCK), jnp.bfloat16),
        in_specs=[pl.BlockSpec(memory_space=pltpu.HBM)] * 4,
        out_specs=vmem,
        scratch_shapes=[
            pltpu.VMEM((BLOCK * BLOCK, BLOCK), jnp.bfloat16),
            pltpu.VMEM((RADIX // 2, 1024, 2 * BLOCK), jnp.bfloat16),
            pltpu.VMEM((FREQS, FREQS), jnp.bfloat16),
            pltpu.VMEM((FREQS, FREQS), jnp.bfloat16),
            pltpu.VMEM((RADIX, 8 * BLOCK, BLOCK), jnp.float32),
            pltpu.SemaphoreType.DMA((FETCHES,)),
            pltpu.SemaphoreType.DMA((3,)),
        ],
        compiler_params=pltpu.CompilerParams(vmem_limit_bytes=VMEM),
        name="front",
    )(
        *[pltpu.with_memory_space_constraint(jnp.asarray(each), pltpu.HBM)
          for each in (rows, dft_tables(), band, order)]
    )


def select(slot_first, slot_second, place, held):
    smem = pl.BlockSpec(memory_space=pltpu.SMEM)
    return pl.pallas_call(
        select_kernel,
        out_shape=jax.ShapeDtypeStruct((128, 96, BLOCK), jnp.bfloat16),
        in_specs=[smem, smem, smem, pl.BlockSpec(memory_space=pltpu.VMEM)],
        scratch_shapes=[pltpu.VMEM((2, NBLK, BLOCK, BLOCK), jnp.bfloat16)],
        compiler_params=pltpu.CompilerParams(vmem_limit_bytes=VMEM),
        name="select",
    )(slot_first, slot_second, place, held)


def correlate(core, own, other):
    vmem = pl.BlockSpec(memory_space=pltpu.VMEM)
    return pl.pallas_call(
        correlate_kernel,
        out_shape=jax.ShapeDtypeStruct((32, SLOT_DEV, BLOCK, LAGS), jnp.float32),
        in_specs=[pl.BlockSpec(memory_space=pltpu.SMEM), vmem, vmem, vmem, vmem],
        out_specs=pl.BlockSpec(memory_space=pl.ANY),
        scratch_shapes=[
            pltpu.VMEM((32, 2 * FREQS // GROUP, GROUP, BLOCK), jnp.bfloat16),
            pltpu.VMEM((SLOT_DEV, 32, BLOCK, LAGS), jnp.float32),
            pltpu.SemaphoreType.DMA((SLOT_DEV, 16 // PAIRS)),
        ],
        compiler_params=pltpu.CompilerParams(vmem_limit_bytes=VMEM),
        name="correlate",
    )(core, own, other, jnp.asarray(group_mask()), jnp.asarray(lag_tables()))


def on_device(traces, pair_offsets, pair_counts, pair_owner):
    slot_first, slot_second = pair_blocks(
        pair_offsets, pair_counts, pair_owner, NBLK, SLOT_DEV * NBLK
    )
    seg = lax.axis_index("seg").astype(jnp.int32).reshape(1)
    held = lax.all_to_all(front(traces), "chan", split_axis=0, concat_axis=0, tiled=True)
    sent = select(slot_first, slot_second, seg, held)
    own = lax.all_to_all(sent, ("chan", "seg"), split_axis=0, concat_axis=0, tiled=True)
    other = lax.ppermute(own[:, :64], "seg", [(0, 1), (1, 0), (2, 3), (3, 2)])
    return correlate(seg % 2, own, other)


def solution(mesh):
    placed = (P("chan", "seg", None), P(), P(), P())
    return jax.shard_map(
        on_device,
        mesh=mesh,
        in_specs=placed,
        out_specs=P("seg", "chan", None, None),
        check_vma=False,
    )
```

```python
import math

import jax
import jax.numpy as jnp
import ml_dtypes
import numpy as np
from jax import lax
from jax.experimental import pallas as pl
from jax.experimental.pallas import tpu as pltpu
from jax.sharding import PartitionSpec as P

SAMPLES = 8192
BAND_START = 32
FREQS = 512
HALF = 8
LAGS = 256
BLOCK = 128
NBLK = 32
SEGS = 8
SLOT_DEV = 2
GROUP = 16
RADIX = 16
VMEM = 32 * 1024 * 1024
PAIRS = 4
UNROLL = 32
FETCHES = 8


def bin_order():
    residues = [(0, 8)] + [(unit, RADIX - unit) for unit in range(1, RADIX // 2)]
    return (np.array(residues)[:, :, None] + RADIX * np.arange(FREQS // RADIX)).reshape(-1)


def dft_tables():
    run = SAMPLES // RADIX
    ring = 2.0 * math.pi / SAMPLES * np.arange(SAMPLES)
    bins = bin_order().reshape(RADIX // 2, 1, 2 * FREQS // RADIX)
    phase = np.arange(run)[None, :, None] * (BAND_START + bins) % SAMPLES
    table = np.concatenate([np.cos(ring)[phase], -np.sin(ring)[phase]], axis=2)
    high = table.astype(np.float32).astype(ml_dtypes.bfloat16)
    low = (table - high.astype(np.float64)).astype(np.float32).astype(ml_dtypes.bfloat16)
    return np.concatenate([high, low], axis=2)


def lag_tables():
    shifts = (np.arange(LAGS) - LAGS // 2) % SAMPLES
    phase = np.outer(BAND_START + np.arange(FREQS), shifts) % SAMPLES
    angles = phase.astype(np.float32) * np.float32(2.0 * math.pi / SAMPLES)
    norm = 1.0 / math.sqrt(FREQS * SEGS)
    parts = np.stack([np.cos(angles), -np.sin(angles)]).astype(ml_dtypes.bfloat16)
    parts = (parts.astype(np.float32) * norm).astype(ml_dtypes.bfloat16)
    parts = parts.reshape(2, FREQS // GROUP, 2, GROUP // 2, LAGS).transpose(4, 1, 0, 2, 3)
    both = np.stack([parts, parts[:, :, :, ::-1]])
    return both.reshape(2, LAGS, 2 * FREQS)


def group_mask():
    lane = np.arange(256)
    own = (lane // 16 % 2) * 8 + lane % 8
    return (np.arange(GROUP)[:, None] == own[None, :]).astype(ml_dtypes.bfloat16)


def pair_blocks(pair_offsets, pair_counts, pair_owner, block_count, slot_count):
    slot_index = lax.iota(jnp.int32, slot_count)
    starts = jnp.cumsum(pair_counts) - pair_counts
    first_block = jnp.sum((starts[None, :] <= slot_index[:, None]).astype(jnp.int32), axis=1) - 1
    member = lax.iota(jnp.int32, block_count)[None, :] == first_block[:, None]
    start_of = jnp.sum(jnp.where(member, starts[None, :], 0), axis=1)
    position = slot_index - start_of
    listed = jnp.sum(jnp.where(member[:, :, None], pair_offsets[None, :, :], 0), axis=1)
    chosen = lax.iota(jnp.int32, pair_offsets.shape[1])[None, :] == position[:, None]
    offset = jnp.sum(jnp.where(chosen, listed, 0), axis=1)
    second_block = jnp.mod(first_block + offset, block_count)
    held = pair_owner[None, :] == slot_index[:, None]
    slot_first = jnp.sum(jnp.where(held, first_block[None, :], 0), axis=1)
    slot_second = jnp.sum(jnp.where(held, second_block[None, :], 0), axis=1)
    return (slot_first, slot_second)


def butterflies(x):
    root, c1, c3 = math.sqrt(0.5), math.cos(math.pi / 8), math.cos(3 * math.pi / 8)
    a = [x[n] + x[n + 8] for n in range(8)]
    b = [x[n] - x[n + 8] for n in range(8)]
    c = [a[n] + a[n + 4] for n in range(4)]
    d = [a[n] - a[n + 4] for n in range(4)]
    even, odd = c[0] + c[2], c[1] + c[3]
    g, h = (d[1] - d[3]) * root, (d[1] + d[3]) * root
    p = [None] + [b[n] - b[8 - n] for n in range(1, 4)]
    q = [None] + [b[n] + b[8 - n] for n in range(1, 4)]
    p2, q2 = p[2] * root, q[2] * root
    re1, re3 = p[1] * c1 + p[3] * c3, p[1] * c3 - p[3] * c1
    im1, im3 = q[1] * c3 + q[3] * c1, q[1] * c1 - q[3] * c3
    plus, minus = b[0] + p2, b[0] - p2
    over, under = q2 + b[4], q2 - b[4]
    return [
        (even + odd, even - odd),
        (plus + re1, im1 + over),
        (d[0] + g, d[2] + h),
        (minus + re3, im3 + under),
        (c[0] - c[2], c[1] - c[3]),
        (minus - re3, im3 - under),
        (d[0] - g, h - d[2]),
        (plus - re1, im1 - over),
    ]


def bin_of(column):
    unit, side, group = column >> 6, (column >> 5) & 1, column & 31
    other = jnp.where(unit == 0, RADIX // 2, RADIX - unit)
    return RADIX * group + jnp.where(side == 0, unit, other)


def front_kernel(
    rows_hbm, dft_hbm, out_ref, rows_ref, dft_ref, band_ref, order_ref, sums_ref, row_sem, table_sem
):
    each = BLOCK * BLOCK // FETCHES
    copies = []
    for fetch in range(FETCHES):
        part = pl.ds(each * fetch, each)
        copies.append(
            pltpu.make_async_copy(rows_hbm.at[part], rows_ref.at[part], row_sem.at[fetch])
        )
        copies[fetch].start()
    table = pltpu.make_async_copy(dft_hbm, dft_ref, table_sem)
    table.start()
    down = lax.broadcasted_iota(jnp.int32, (FREQS, BLOCK), 0)
    across = lax.broadcasted_iota(jnp.int32, (FREQS, BLOCK), 1)
    bins = bin_of(down)
    for tile in range(FREQS // BLOCK):
        lanes = slice(tile * BLOCK, (tile + 1) * BLOCK)
        column = bin_of(across[:8] + tile * BLOCK)[:1]
        near = jnp.abs(bins - column) <= HALF
        band_ref[:, lanes] = jnp.where(near, 1.0, 0.0).astype(jnp.bfloat16)
        order_ref[:, lanes] = jnp.where(down == column, 1.0, 0.0).astype(jnp.bfloat16)

    def channel(chan, carry):
        x = []
        for pair in range(RADIX // 2):
            tile = rows_ref[pl.ds(pl.multiple_of(BLOCK * chan + 16 * pair, 16), 16), :]
            tile = tile.astype(jnp.float32)
            x += [tile[:8], tile[8:]]
        for unit, sums in enumerate(butterflies(x)):
            for side in range(2):
                sums_ref[2 * unit + side, pl.ds(pl.multiple_of(8 * chan, 8), 8), :] = sums[side]
        return carry

    for fetch in range(FETCHES):
        copies[fetch].wait()
        count = BLOCK // FETCHES
        lax.fori_loop(count * fetch, count * (fetch + 1), channel, 0, unroll=4)

    lane = lax.broadcasted_iota(jnp.int32, (1, BLOCK), 1)
    sign = jnp.where((lane < 32) | (lane >= 96), 1.0, -1.0)
    table.wait()
    found = []
    for unit in range(RADIX // 2):
        tiles = []
        for side in range(2):
            for seg in range(2):
                tiles.append(
                    jnp.concatenate(
                        [
                            sums_ref[2 * unit + side, pl.ds(2 * tile + seg, BLOCK, stride=8), :]
                            for tile in range(4)
                        ],
                        axis=1,
                    )
                )
        exact = jnp.concatenate(tiles, axis=0)
        high = exact.astype(jnp.bfloat16)
        low = (exact - high.astype(jnp.float32)).astype(jnp.bfloat16)
        first = jnp.dot(high, dft_ref[unit], preferred_element_type=jnp.float32)
        rest = jnp.dot(low, dft_ref[unit, :, :BLOCK], preferred_element_type=jnp.float32)
        both = first[:, :BLOCK] + (first[:, BLOCK:] + rest)
        one, two = both[: 2 * BLOCK], both[2 * BLOCK :]
        if unit == 0:
            found.append(jnp.where((lane >> 5) & 1 == 0, one, two))
        else:
            found.append(one + sign * pltpu.roll(two, 64, 1))
    left = lax.broadcasted_iota(jnp.int32, (2 * BLOCK, BLOCK), 1) < 64
    real = []
    imag = []
    for one, two in zip(found[0::2], found[1::2]):
        real.append(jnp.where(left, one, pltpu.roll(two, 64, 1)))
        imag.append(jnp.where(left, pltpu.roll(one, 64, 1), two))
    real = jnp.concatenate(real, axis=1)
    imag = jnp.concatenate(imag, axis=1)
    amplitude = jnp.sqrt(real * real + imag * imag)
    high = amplitude.astype(jnp.bfloat16)
    low = (amplitude - high.astype(jnp.float32)).astype(jnp.bfloat16)
    band = band_ref[...]
    total = jnp.dot(high, band, preferred_element_type=jnp.float32)
    total = total + jnp.dot(low, band, preferred_element_type=jnp.float32)
    count = jnp.dot(jnp.ones((8, FREQS), jnp.bfloat16), band, preferred_element_type=jnp.float32)
    divisor = jnp.maximum(total / count[:1], 1.0)
    for part, spectrum in enumerate([real, imag]):
        white = (spectrum / divisor).astype(jnp.bfloat16)
        turned = lax.dot_general(
            order_ref[...], white, (((1,), (1,)), ((), ())), preferred_element_type=jnp.float32
        )
        pieces = [
            turned[:, BLOCK * seg : BLOCK * (seg + 1)].reshape(FREQS // 8, 1, 8, BLOCK)
            for seg in range(2)
        ]
        both = jnp.concatenate(pieces, axis=1).reshape(NBLK, 2 * GROUP, BLOCK)
        out_ref[:, part * 2 * GROUP : (part + 1) * 2 * GROUP, :] = both.astype(jnp.bfloat16)


def select_kernel(first_ref, second_ref, place_ref, held_ref, out_ref, rows_ref):
    lane = lax.broadcasted_iota(jnp.int32, (32, BLOCK), 1)
    left = (lane < 64) == (place_ref[0] % 2 == 0)

    def turn(block, carry):
        tiles = held_ref[block].astype(jnp.float32)
        for core in range(2):
            order = tiles if core == 0 else jnp.concatenate(
                [tiles[16:32], tiles[0:16], tiles[48:64], tiles[32:48]], axis=0
            )
            twice = jnp.concatenate([order, order], axis=0)
            rows_ref[core, block] = twice.T.astype(jnp.bfloat16)
        return carry

    lax.fori_loop(0, NBLK, turn, 0, unroll=8)

    def send(chan, carry):
        slots = [SLOT_DEV * chan + slot for slot in range(SLOT_DEV)]
        for seg in range(4):
            core = seg % 2
            dest = 4 * chan + seg
            for slot in range(SLOT_DEV):
                second = second_ref[slots[slot]]
                for part in range(2):
                    out_ref[dest, pl.ds(32 * slot + 16 * part, 16), :] = held_ref[
                        second, pl.ds(32 * part + 16 * core, 16), :
                    ]
            one = rows_ref[core, first_ref[slots[0]], pl.ds(32 * seg, 32), :]
            two = rows_ref[core, first_ref[slots[1]], pl.ds(32 * seg, 32), :]
            out_ref[dest, pl.ds(64, 32), :] = jnp.where(left, one, two)
        return carry

    lax.fori_loop(0, NBLK, send, 0, unroll=8)


def correlate_kernel(
    core_ref, own_ref, other_ref, mask_ref, table_ref, out_hbm, cross_ref, lag_ref, out_sem
):
    core = core_ref[0]
    leaving = []
    for slot in range(SLOT_DEV):

        def cross(group, carry):
            order = [slot, 1 - slot, 2 + slot, 3 - slot]
            upper = []
            lower = []
            for seg in order:
                src = 4 * group + seg
                tiles = []
                for part in range(2):
                    rows = pl.ds(32 * slot + 16 * part, 16)
                    tiles.append([own_ref[src, rows, :], other_ref[src, rows, :]])
                upper += tiles[0] + tiles[1]
                lower += [-tiles[1][0], -tiles[1][1]] + tiles[0]
            second = jnp.concatenate(
                [jnp.concatenate(upper, axis=0), jnp.concatenate(lower, axis=0)], axis=1
            )
            lane = lax.broadcasted_iota(jnp.int32, (32, BLOCK), 1)
            left = (lane < 64) == (slot == 0)
            lanes = [own_ref[4 * group + seg, pl.ds(64, 32), :] for seg in range(4)]
            first = jnp.concatenate(
                [jnp.where(left, lanes[0], lanes[1]), jnp.where(left, lanes[2], lanes[3])], axis=1
            )
            mask = mask_ref[...]
            spread = [jnp.broadcast_to(first[i : i + 1], (GROUP, 256)) * mask for i in range(32)]
            found = jnp.dot(
                jnp.concatenate(spread, axis=0), second, preferred_element_type=jnp.float32
            ).astype(jnp.bfloat16)
            for part in range(2):
                cross_ref[:, 2 * group + part] = found[
                    :, part * BLOCK : (part + 1) * BLOCK
                ].reshape(32, GROUP, BLOCK)
            return carry

        def lags(pair, carry):
            sides = [cross_ref[2 * pair + k].reshape(2 * FREQS, BLOCK) for k in range(2)]
            lagged = jnp.dot(
                table_ref[core], jnp.concatenate(sides, axis=1), preferred_element_type=jnp.float32
            )
            for k in range(2):
                lag_ref[slot, 2 * pair + k] = lagged[:, k * BLOCK : (k + 1) * BLOCK].T
            return carry

        lax.fori_loop(0, NBLK, cross, 0, unroll=UNROLL)
        for step in range(16 // PAIRS):
            lax.fori_loop(PAIRS * step, PAIRS * (step + 1), lags, 0, unroll=True)
            rows = pl.ds(2 * PAIRS * step, 2 * PAIRS)
            copy = pltpu.make_async_copy(
                lag_ref.at[slot, rows], out_hbm.at[rows, slot], out_sem.at[slot, step]
            )
            copy.start()
            leaving.append(copy)
    for copy in leaving:
        copy.wait()


def front(traces):
    rows = traces.reshape(BLOCK, 2, SAMPLES // BLOCK, BLOCK).transpose(0, 2, 1, 3)
    rows = rows.reshape(BLOCK * BLOCK, BLOCK)
    return pl.pallas_call(
        front_kernel,
        out_shape=jax.ShapeDtypeStruct((NBLK, 4 * GROUP, BLOCK), jnp.bfloat16),
        in_specs=[pl.BlockSpec(memory_space=pltpu.HBM)] * 2,
        out_specs=pl.BlockSpec(memory_space=pltpu.VMEM),
        scratch_shapes=[
            pltpu.VMEM((BLOCK * BLOCK, BLOCK), jnp.bfloat16),
            pltpu.VMEM((RADIX // 2, SAMPLES // RADIX, 2 * BLOCK), jnp.bfloat16),
            pltpu.VMEM((FREQS, FREQS), jnp.bfloat16),
            pltpu.VMEM((FREQS, FREQS), jnp.bfloat16),
            pltpu.VMEM((RADIX, 8 * BLOCK, BLOCK), jnp.float32),
            pltpu.SemaphoreType.DMA((FETCHES,)),
            pltpu.SemaphoreType.DMA,
        ],
        compiler_params=pltpu.CompilerParams(vmem_limit_bytes=VMEM),
        name="front",
    )(
        pltpu.with_memory_space_constraint(rows, pltpu.HBM),
        pltpu.with_memory_space_constraint(jnp.asarray(dft_tables()), pltpu.HBM),
    )


def select(slot_first, slot_second, place, held):
    smem = pl.BlockSpec(memory_space=pltpu.SMEM)
    return pl.pallas_call(
        select_kernel,
        out_shape=jax.ShapeDtypeStruct((128, 96, BLOCK), jnp.bfloat16),
        in_specs=[smem, smem, smem, pl.BlockSpec(memory_space=pltpu.VMEM)],
        scratch_shapes=[pltpu.VMEM((2, NBLK, BLOCK, BLOCK), jnp.bfloat16)],
        compiler_params=pltpu.CompilerParams(vmem_limit_bytes=VMEM),
        name="select",
    )(slot_first, slot_second, place, held)


def correlate(core, own, other):
    vmem = pl.BlockSpec(memory_space=pltpu.VMEM)
    return pl.pallas_call(
        correlate_kernel,
        out_shape=jax.ShapeDtypeStruct((32, SLOT_DEV, BLOCK, LAGS), jnp.float32),
        in_specs=[pl.BlockSpec(memory_space=pltpu.SMEM), vmem, vmem, vmem, vmem],
        out_specs=pl.BlockSpec(memory_space=pl.ANY),
        scratch_shapes=[
            pltpu.VMEM((32, 2 * FREQS // GROUP, GROUP, BLOCK), jnp.bfloat16),
            pltpu.VMEM((SLOT_DEV, 32, BLOCK, LAGS), jnp.float32),
            pltpu.SemaphoreType.DMA((SLOT_DEV, 16 // PAIRS)),
        ],
        compiler_params=pltpu.CompilerParams(vmem_limit_bytes=VMEM),
        name="correlate",
    )(core, own, other, jnp.asarray(group_mask()), jnp.asarray(lag_tables()))


def on_device(traces, pair_offsets, pair_counts, pair_owner):
    slot_first, slot_second = pair_blocks(
        pair_offsets, pair_counts, pair_owner, NBLK, SLOT_DEV * NBLK
    )
    seg = lax.axis_index("seg").astype(jnp.int32).reshape(1)
    held = lax.all_to_all(front(traces), "chan", split_axis=0, concat_axis=0, tiled=True)
    sent = select(slot_first, slot_second, seg, held)
    own = lax.all_to_all(sent, ("chan", "seg"), split_axis=0, concat_axis=0, tiled=True)
    other = lax.ppermute(own[:, :64], "seg", [(0, 1), (1, 0), (2, 3), (3, 2)])
    return correlate(seg % 2, own, other)


def solution(mesh):
    placed = (P("chan", "seg", None), P(), P(), P())
    return jax.shard_map(
        on_device,
        mesh=mesh,
        in_specs=placed,
        out_specs=P("seg", "chan", None, None),
        check_vma=False,
    )
```

```python
import math

import jax
import jax.numpy as jnp
import ml_dtypes
import numpy as np
from jax import lax
from jax.experimental import pallas as pl
from jax.experimental.pallas import tpu as pltpu
from jax.sharding import PartitionSpec as P

SAMPLES = 8192
BAND_START = 32
FREQS = 512
HALF = 8
LAGS = 256
BLOCK = 128
NBLK = 32
SEGS = 8
SLOT_DEV = 2
GROUP = 16
RADIX = 16
VMEM = 32 * 1024 * 1024
PAIRS = 4
UNROLL = 16
FETCHES = 8


def bin_order():
    residues = [(0, 8)] + [(unit, RADIX - unit) for unit in range(1, RADIX // 2)]
    return (np.array(residues)[:, :, None] + RADIX * np.arange(FREQS // RADIX)).reshape(-1)


def dft_tables():
    run = SAMPLES // RADIX
    ring = 2.0 * math.pi / SAMPLES * np.arange(SAMPLES)
    bins = bin_order().reshape(RADIX // 2, 1, 2 * FREQS // RADIX)
    phase = np.arange(run)[None, :, None] * (BAND_START + bins) % SAMPLES
    table = np.concatenate([np.cos(ring)[phase], -np.sin(ring)[phase]], axis=2)
    high = table.astype(np.float32).astype(ml_dtypes.bfloat16)
    low = (table - high.astype(np.float64)).astype(np.float32).astype(ml_dtypes.bfloat16)
    return np.concatenate([high, low], axis=2)


def lag_tables():
    shifts = (np.arange(LAGS) - LAGS // 2) % SAMPLES
    phase = np.outer(BAND_START + np.arange(FREQS), shifts) % SAMPLES
    angles = phase.astype(np.float32) * np.float32(2.0 * math.pi / SAMPLES)
    norm = 1.0 / math.sqrt(FREQS * SEGS)
    parts = np.stack([np.cos(angles), -np.sin(angles)]).astype(ml_dtypes.bfloat16)
    parts = (parts.astype(np.float32) * norm).astype(ml_dtypes.bfloat16)
    parts = parts.reshape(2, NBLK // 2, 2, 2, GROUP // 2, LAGS).transpose(5, 3, 1, 0, 2, 4)
    both = np.stack([parts, parts[:, ::-1]])
    return both.reshape(2, LAGS, 2 * FREQS)


def group_mask():
    lane, row = np.arange(256)[None, :], np.arange(GROUP)[:, None]
    same = (lane // 128 == row // 8) & (lane % 8 == row % 8)
    return same.astype(ml_dtypes.bfloat16)


def pair_blocks(pair_offsets, pair_counts, pair_owner, block_count, slot_count):
    slot_index = lax.iota(jnp.int32, slot_count)
    starts = jnp.cumsum(pair_counts) - pair_counts
    first_block = jnp.sum((starts[None, :] <= slot_index[:, None]).astype(jnp.int32), axis=1) - 1
    member = lax.iota(jnp.int32, block_count)[None, :] == first_block[:, None]
    start_of = jnp.sum(jnp.where(member, starts[None, :], 0), axis=1)
    position = slot_index - start_of
    listed = jnp.sum(jnp.where(member[:, :, None], pair_offsets[None, :, :], 0), axis=1)
    chosen = lax.iota(jnp.int32, pair_offsets.shape[1])[None, :] == position[:, None]
    offset = jnp.sum(jnp.where(chosen, listed, 0), axis=1)
    second_block = jnp.mod(first_block + offset, block_count)
    held = pair_owner[None, :] == slot_index[:, None]
    slot_first = jnp.sum(jnp.where(held, first_block[None, :], 0), axis=1)
    slot_second = jnp.sum(jnp.where(held, second_block[None, :], 0), axis=1)
    return (slot_first, slot_second)


def butterflies(x):
    root, c1, c3 = math.sqrt(0.5), math.cos(math.pi / 8), math.cos(3 * math.pi / 8)
    a = [x[n] + x[n + 8] for n in range(8)]
    b = [x[n] - x[n + 8] for n in range(8)]
    c = [a[n] + a[n + 4] for n in range(4)]
    d = [a[n] - a[n + 4] for n in range(4)]
    even, odd = c[0] + c[2], c[1] + c[3]
    g, h = (d[1] - d[3]) * root, (d[1] + d[3]) * root
    p = [None] + [b[n] - b[8 - n] for n in range(1, 4)]
    q = [None] + [b[n] + b[8 - n] for n in range(1, 4)]
    p2, q2 = p[2] * root, q[2] * root
    re1, re3 = p[1] * c1 + p[3] * c3, p[1] * c3 - p[3] * c1
    im1, im3 = q[1] * c3 + q[3] * c1, q[1] * c1 - q[3] * c3
    plus, minus = b[0] + p2, b[0] - p2
    over, under = q2 + b[4], q2 - b[4]
    return [
        (even + odd, even - odd),
        (plus + re1, im1 + over),
        (d[0] + g, d[2] + h),
        (minus + re3, im3 + under),
        (c[0] - c[2], c[1] - c[3]),
        (minus - re3, im3 - under),
        (d[0] - g, h - d[2]),
        (plus - re1, im1 - over),
    ]


def bin_of(column):
    unit, side, group = column >> 6, (column >> 5) & 1, column & 31
    other = jnp.where(unit == 0, RADIX // 2, RADIX - unit)
    return RADIX * group + jnp.where(side == 0, unit, other)


def front_kernel(
    rows_hbm, dft_hbm, out_ref, rows_ref, dft_ref, band_ref, order_ref, sums_ref, row_sem, table_sem
):
    each = BLOCK * BLOCK // FETCHES
    copies = []
    for fetch in range(FETCHES):
        part = pl.ds(each * fetch, each)
        copies.append(
            pltpu.make_async_copy(rows_hbm.at[part], rows_ref.at[part], row_sem.at[fetch])
        )
        copies[fetch].start()
    table = pltpu.make_async_copy(dft_hbm, dft_ref, table_sem)
    table.start()
    down = lax.broadcasted_iota(jnp.int32, (FREQS, BLOCK), 0)
    across = lax.broadcasted_iota(jnp.int32, (FREQS, BLOCK), 1)
    bins = bin_of(down)
    for tile in range(FREQS // BLOCK):
        lanes = slice(tile * BLOCK, (tile + 1) * BLOCK)
        column = bin_of(across[:8] + tile * BLOCK)[:1]
        near = jnp.abs(bins - column) <= HALF
        band_ref[:, lanes] = jnp.where(near, 1.0, 0.0).astype(jnp.bfloat16)
        order_ref[:, lanes] = jnp.where(down == column, 1.0, 0.0).astype(jnp.bfloat16)

    def channel(chan, carry):
        x = []
        for pair in range(RADIX // 2):
            tile = rows_ref[pl.ds(pl.multiple_of(BLOCK * chan + 16 * pair, 16), 16), :]
            tile = tile.astype(jnp.float32)
            x += [tile[:8], tile[8:]]
        for unit, sums in enumerate(butterflies(x)):
            for side in range(2):
                sums_ref[2 * unit + side, pl.ds(pl.multiple_of(8 * chan, 8), 8), :] = sums[side]
        return carry

    for fetch in range(FETCHES):
        copies[fetch].wait()
        count = BLOCK // FETCHES
        lax.fori_loop(count * fetch, count * (fetch + 1), channel, 0, unroll=4)

    lane = lax.broadcasted_iota(jnp.int32, (1, BLOCK), 1)
    sign = jnp.where((lane < 32) | (lane >= 96), 1.0, -1.0)
    table.wait()
    found = []
    for unit in range(RADIX // 2):
        tiles = []
        for side in range(2):
            for seg in range(2):
                tiles.append(
                    jnp.concatenate(
                        [
                            sums_ref[2 * unit + side, pl.ds(2 * tile + seg, BLOCK, stride=8), :]
                            for tile in range(4)
                        ],
                        axis=1,
                    )
                )
        exact = jnp.concatenate(tiles, axis=0)
        high = exact.astype(jnp.bfloat16)
        low = (exact - high.astype(jnp.float32)).astype(jnp.bfloat16)
        first = jnp.dot(high, dft_ref[unit], preferred_element_type=jnp.float32)
        rest = jnp.dot(low, dft_ref[unit, :, :BLOCK], preferred_element_type=jnp.float32)
        both = first[:, :BLOCK] + (first[:, BLOCK:] + rest)
        one, two = both[: 2 * BLOCK], both[2 * BLOCK :]
        if unit == 0:
            found.append(jnp.where((lane >> 5) & 1 == 0, one, two))
        else:
            found.append(one + sign * pltpu.roll(two, 64, 1))
    left = lax.broadcasted_iota(jnp.int32, (2 * BLOCK, BLOCK), 1) < 64
    real = []
    imag = []
    for one, two in zip(found[0::2], found[1::2]):
        real.append(jnp.where(left, one, pltpu.roll(two, 64, 1)))
        imag.append(jnp.where(left, pltpu.roll(one, 64, 1), two))
    real = jnp.concatenate(real, axis=1)
    imag = jnp.concatenate(imag, axis=1)
    amplitude = jnp.sqrt(real * real + imag * imag)
    high = amplitude.astype(jnp.bfloat16)
    low = (amplitude - high.astype(jnp.float32)).astype(jnp.bfloat16)
    band = band_ref[...]
    total = jnp.dot(high, band, preferred_element_type=jnp.float32)
    total = total + jnp.dot(low, band, preferred_element_type=jnp.float32)
    count = jnp.dot(jnp.ones((8, FREQS), jnp.bfloat16), band, preferred_element_type=jnp.float32)
    divisor = jnp.maximum(total / count[:1], 1.0)
    for part, spectrum in enumerate([real, imag]):
        white = (spectrum / divisor).astype(jnp.bfloat16)
        turned = lax.dot_general(
            order_ref[...], white, (((1,), (1,)), ((), ())), preferred_element_type=jnp.float32
        )
        pieces = [
            turned[:, BLOCK * seg : BLOCK * (seg + 1)].reshape(FREQS // 8, 1, 8, BLOCK)
            for seg in range(2)
        ]
        both = jnp.concatenate(pieces, axis=1).reshape(NBLK, 2 * GROUP, BLOCK)
        out_ref[:, part * 2 * GROUP : (part + 1) * 2 * GROUP, :] = both.astype(jnp.bfloat16)


def select_kernel(first_ref, second_ref, place_ref, held_ref, out_ref, rows_ref):
    lane = lax.broadcasted_iota(jnp.int32, (32, BLOCK), 1)
    place = place_ref[0]
    left = (((lane >> 5) - place) & 3) < 2

    def turn(block, carry):
        tiles = held_ref[block].astype(jnp.float32)
        halves = [[tiles[0:16], tiles[32:48]], [tiles[16:32], tiles[48:64]]]
        for lead in range(2):
            order = halves[lead] + halves[1 - lead]
            rows_ref[lead, block] = jnp.concatenate(order + order, axis=0).T.astype(jnp.bfloat16)
        return carry

    lax.fori_loop(0, NBLK, turn, 0, unroll=8)

    def send(chan, carry):
        slots = [SLOT_DEV * chan + slot for slot in range(SLOT_DEV)]
        for seg in range(4):
            core = seg % 2
            dest = 4 * chan + seg
            for slot in range(SLOT_DEV):
                second = second_ref[slots[slot]]
                for part in range(2):
                    out_ref[dest, pl.ds(32 * slot + 16 * part, 16), :] = held_ref[
                        second, pl.ds(32 * part + 16 * core, 16), :
                    ]
            lead = (place & 1) ^ core
            one = rows_ref[lead, first_ref[slots[0]], pl.ds(32 * seg, 32), :]
            two = rows_ref[lead, first_ref[slots[1]], pl.ds(32 * seg, 32), :]
            out_ref[dest, pl.ds(64, 32), :] = jnp.where(left, one, two)
        return carry

    lax.fori_loop(0, NBLK, send, 0, unroll=8)


def cross_of(slot, half, pair, second_ref, own_ref, mask):
    lane = lax.broadcasted_iota(jnp.int32, (32, BLOCK), 1) >> 5
    place = 2 * slot + half
    upper = []
    lower = []
    first = []
    for group in range(2):
        lanes = None
        for block in range(4):
            src = 8 * pair + 4 * group + (block - place) % 4
            real = second_ref[src, pl.ds(32 * slot, 16), :]
            imag = second_ref[src, pl.ds(32 * slot + 16, 16), :]
            upper += [real, imag]
            lower += [-imag, real]
            piece = own_ref[src, pl.ds(64, 32), :]
            lanes = piece if lanes is None else jnp.where(lane == block, piece, lanes)
        first.append(lanes)
    second = jnp.concatenate(
        [jnp.concatenate(upper, axis=0), jnp.concatenate(lower, axis=0)], axis=1
    )
    first = jnp.concatenate(first, axis=1)
    spread = [jnp.broadcast_to(first[i : i + 1], (GROUP, 256)) * mask for i in range(32)]
    found = jnp.dot(
        jnp.concatenate(spread, axis=0), second, preferred_element_type=jnp.float32
    ).astype(jnp.bfloat16)
    return [
        found[:, part * BLOCK : (part + 1) * BLOCK].reshape(32, GROUP, BLOCK) for part in range(2)
    ]


def near_kernel(own_ref, mask_ref, cross_ref):
    for slot in range(SLOT_DEV):

        def cross(pair, carry):
            for part, found in enumerate(cross_of(slot, 0, pair, own_ref, own_ref, mask_ref[...])):
                cross_ref[slot, :, 2 * pair + part] = found
            return carry

        lax.fori_loop(0, NBLK // 2, cross, 0, unroll=UNROLL)


def correlate_kernel(
    core_ref, own_ref, other_ref, near_ref, mask_ref, table_ref, out_hbm, cross_ref, lag_ref, out_sem
):
    core = core_ref[0]
    leaving = []
    for slot in range(SLOT_DEV):

        def cross(pair, carry):
            for part, found in enumerate(
                cross_of(slot, 1, pair, other_ref, own_ref, mask_ref[...])
            ):
                cross_ref[:, 2 * pair + part] = found
            return carry

        def lags(pair, carry):
            sides = []
            for k in range(2):
                near = near_ref[slot, 2 * pair + k].reshape(FREQS, BLOCK)
                far = cross_ref[2 * pair + k].reshape(FREQS, BLOCK)
                sides.append(jnp.concatenate([near, far], axis=0))
            lagged = jnp.dot(
                table_ref[core], jnp.concatenate(sides, axis=1), preferred_element_type=jnp.float32
            )
            both = lagged.T
            for k in range(2):
                lag_ref[slot, 2 * pair + k] = both[k * BLOCK : (k + 1) * BLOCK]
            return carry

        lax.fori_loop(0, NBLK // 2, cross, 0, unroll=UNROLL)
        for step in range(16 // PAIRS):
            lax.fori_loop(PAIRS * step, PAIRS * (step + 1), lags, 0, unroll=True)
            rows = pl.ds(2 * PAIRS * step, 2 * PAIRS)
            copy = pltpu.make_async_copy(
                lag_ref.at[slot, rows], out_hbm.at[rows, slot], out_sem.at[slot, step]
            )
            copy.start()
            leaving.append(copy)
    for copy in leaving:
        copy.wait()


def front(traces):
    rows = traces.reshape(BLOCK, 2, SAMPLES // BLOCK, BLOCK).transpose(0, 2, 1, 3)
    rows = rows.reshape(BLOCK * BLOCK, BLOCK)
    return pl.pallas_call(
        front_kernel,
        out_shape=jax.ShapeDtypeStruct((NBLK, 4 * GROUP, BLOCK), jnp.bfloat16),
        in_specs=[pl.BlockSpec(memory_space=pltpu.HBM)] * 2,
        out_specs=pl.BlockSpec(memory_space=pltpu.VMEM),
        scratch_shapes=[
            pltpu.VMEM((BLOCK * BLOCK, BLOCK), jnp.bfloat16),
            pltpu.VMEM((RADIX // 2, SAMPLES // RADIX, 2 * BLOCK), jnp.bfloat16),
            pltpu.VMEM((FREQS, FREQS), jnp.bfloat16),
            pltpu.VMEM((FREQS, FREQS), jnp.bfloat16),
            pltpu.VMEM((RADIX, 8 * BLOCK, BLOCK), jnp.float32),
            pltpu.SemaphoreType.DMA((FETCHES,)),
            pltpu.SemaphoreType.DMA,
        ],
        compiler_params=pltpu.CompilerParams(vmem_limit_bytes=VMEM),
        name="front",
    )(
        pltpu.with_memory_space_constraint(rows, pltpu.HBM),
        pltpu.with_memory_space_constraint(jnp.asarray(dft_tables()), pltpu.HBM),
    )


def select(slot_first, slot_second, place, held):
    smem = pl.BlockSpec(memory_space=pltpu.SMEM)
    return pl.pallas_call(
        select_kernel,
        out_shape=jax.ShapeDtypeStruct((128, 96, BLOCK), jnp.bfloat16),
        in_specs=[smem, smem, smem, pl.BlockSpec(memory_space=pltpu.VMEM)],
        scratch_shapes=[pltpu.VMEM((2, NBLK, BLOCK, BLOCK), jnp.bfloat16)],
        compiler_params=pltpu.CompilerParams(vmem_limit_bytes=VMEM),
        name="select",
    )(slot_first, slot_second, place, held)


def near_cross(own):
    vmem = pl.BlockSpec(memory_space=pltpu.VMEM)
    return pl.pallas_call(
        near_kernel,
        out_shape=jax.ShapeDtypeStruct((SLOT_DEV, 32, NBLK, GROUP, BLOCK), jnp.bfloat16),
        in_specs=[vmem, vmem],
        out_specs=vmem,
        compiler_params=pltpu.CompilerParams(vmem_limit_bytes=16 * 1024 * 1024),
        cost_estimate=pl.CostEstimate(flops=8 << 30, transcendentals=0, bytes_accessed=11 << 20),
        name="near_cross",
    )(own, jnp.asarray(group_mask()))


def correlate(core, own, other, near=None):
    near = near_cross(own) if near is None else near
    vmem = pl.BlockSpec(memory_space=pltpu.VMEM)
    return pl.pallas_call(
        correlate_kernel,
        out_shape=jax.ShapeDtypeStruct((32, SLOT_DEV, BLOCK, LAGS), jnp.float32),
        in_specs=[pl.BlockSpec(memory_space=pltpu.SMEM)] + [vmem] * 5,
        out_specs=pl.BlockSpec(memory_space=pl.ANY),
        scratch_shapes=[
            pltpu.VMEM((32, NBLK, GROUP, BLOCK), jnp.bfloat16),
            pltpu.VMEM((SLOT_DEV, 32, BLOCK, LAGS), jnp.float32),
            pltpu.SemaphoreType.DMA((SLOT_DEV, 16 // PAIRS)),
        ],
        compiler_params=pltpu.CompilerParams(vmem_limit_bytes=24 * 1024 * 1024),
        name="correlate",
    )(core, own, other, near, jnp.asarray(group_mask()), jnp.asarray(lag_tables()))


def on_device(traces, pair_offsets, pair_counts, pair_owner):
    slot_first, slot_second = pair_blocks(
        pair_offsets, pair_counts, pair_owner, NBLK, SLOT_DEV * NBLK
    )
    seg = lax.axis_index("seg").astype(jnp.int32).reshape(1)
    held = lax.all_to_all(front(traces), "chan", split_axis=0, concat_axis=0, tiled=True)
    sent = select(slot_first, slot_second, seg, held)
    own = lax.all_to_all(sent, ("chan", "seg"), split_axis=0, concat_axis=0, tiled=True)
    other = lax.ppermute(own[:, :64], "seg", [(0, 1), (1, 0), (2, 3), (3, 2)])
    return correlate(seg % 2, own, other, near_cross(own))


def solution(mesh):
    placed = (P("chan", "seg", None), P(), P(), P())
    return jax.shard_map(
        on_device,
        mesh=mesh,
        in_specs=placed,
        out_specs=P("seg", "chan", None, None),
        check_vma=False,
    )
```

```python
import math

import jax
import jax.numpy as jnp
import ml_dtypes
import numpy as np
from jax import lax
from jax.experimental import pallas as pl
from jax.experimental.pallas import tpu as pltpu
from jax.sharding import PartitionSpec as P

SAMPLES = 8192
BAND_START = 32
FREQS = 512
HALF = 8
LAGS = 256
BLOCK = 128
NBLK = 32
SEGS = 8
SLOT_DEV = 2
GROUP = 16
RADIX = 16
VMEM = 32 * 1024 * 1024
PAIRS = 4
UNROLL = 16
FETCHES = 8


def bin_order():
    residues = [(0, 8)] + [(unit, RADIX - unit) for unit in range(1, RADIX // 2)]
    return (np.array(residues)[:, :, None] + RADIX * np.arange(FREQS // RADIX)).reshape(-1)


def dft_tables():
    run = SAMPLES // RADIX
    ring = 2.0 * math.pi / SAMPLES * np.arange(SAMPLES)
    bins = bin_order().reshape(RADIX // 2, 1, 2 * FREQS // RADIX)
    phase = np.arange(run)[None, :, None] * (BAND_START + bins) % SAMPLES
    table = np.concatenate([np.cos(ring)[phase], -np.sin(ring)[phase]], axis=2)
    high = table.astype(np.float32).astype(ml_dtypes.bfloat16)
    low = (table - high.astype(np.float64)).astype(np.float32).astype(ml_dtypes.bfloat16)
    return np.concatenate([high, low], axis=2)


def lag_tables():
    shifts = (np.arange(LAGS) - LAGS // 2) % SAMPLES
    phase = np.outer(BAND_START + np.arange(FREQS), shifts) % SAMPLES
    angles = phase.astype(np.float32) * np.float32(2.0 * math.pi / SAMPLES)
    norm = 1.0 / math.sqrt(FREQS * SEGS)
    parts = np.stack([np.cos(angles), -np.sin(angles)]).astype(ml_dtypes.bfloat16)
    parts = (parts.astype(np.float32) * norm).astype(ml_dtypes.bfloat16)
    parts = parts.reshape(2, NBLK // 2, 2, 2, GROUP // 2, LAGS).transpose(5, 3, 1, 0, 2, 4)
    both = np.stack([parts, parts[:, ::-1]])
    return both.reshape(2, LAGS, 2 * FREQS)


def group_mask():
    lane, row = np.arange(256)[None, :], np.arange(GROUP)[:, None]
    same = (lane // 128 == row // 8) & (lane % 8 == row % 8)
    return same.astype(ml_dtypes.bfloat16)


def pair_blocks(pair_offsets, pair_counts, pair_owner, block_count, slot_count):
    slot_index = lax.iota(jnp.int32, slot_count)
    starts = jnp.cumsum(pair_counts) - pair_counts
    first_block = jnp.sum((starts[None, :] <= slot_index[:, None]).astype(jnp.int32), axis=1) - 1
    member = lax.iota(jnp.int32, block_count)[None, :] == first_block[:, None]
    start_of = jnp.sum(jnp.where(member, starts[None, :], 0), axis=1)
    position = slot_index - start_of
    listed = jnp.sum(jnp.where(member[:, :, None], pair_offsets[None, :, :], 0), axis=1)
    chosen = lax.iota(jnp.int32, pair_offsets.shape[1])[None, :] == position[:, None]
    offset = jnp.sum(jnp.where(chosen, listed, 0), axis=1)
    second_block = jnp.mod(first_block + offset, block_count)
    held = pair_owner[None, :] == slot_index[:, None]
    slot_first = jnp.sum(jnp.where(held, first_block[None, :], 0), axis=1)
    slot_second = jnp.sum(jnp.where(held, second_block[None, :], 0), axis=1)
    return (slot_first, slot_second)


def butterflies(x):
    root, c1, c3 = math.sqrt(0.5), math.cos(math.pi / 8), math.cos(3 * math.pi / 8)
    a = [x[n] + x[n + 8] for n in range(8)]
    b = [x[n] - x[n + 8] for n in range(8)]
    c = [a[n] + a[n + 4] for n in range(4)]
    d = [a[n] - a[n + 4] for n in range(4)]
    even, odd = c[0] + c[2], c[1] + c[3]
    g, h = (d[1] - d[3]) * root, (d[1] + d[3]) * root
    p = [None] + [b[n] - b[8 - n] for n in range(1, 4)]
    q = [None] + [b[n] + b[8 - n] for n in range(1, 4)]
    p2, q2 = p[2] * root, q[2] * root
    re1, re3 = p[1] * c1 + p[3] * c3, p[1] * c3 - p[3] * c1
    im1, im3 = q[1] * c3 + q[3] * c1, q[1] * c1 - q[3] * c3
    plus, minus = b[0] + p2, b[0] - p2
    over, under = q2 + b[4], q2 - b[4]
    return [
        (even + odd, even - odd),
        (plus + re1, im1 + over),
        (d[0] + g, d[2] + h),
        (minus + re3, im3 + under),
        (c[0] - c[2], c[1] - c[3]),
        (minus - re3, im3 - under),
        (d[0] - g, h - d[2]),
        (plus - re1, im1 - over),
    ]


def bin_of(column):
    unit, side, group = column >> 6, (column >> 5) & 1, column & 31
    other = jnp.where(unit == 0, RADIX // 2, RADIX - unit)
    return RADIX * group + jnp.where(side == 0, unit, other)


def front_kernel(
    rows_hbm, dft_hbm, out_ref, rows_ref, dft_ref, band_ref, order_ref, sums_ref, row_sem, table_sem
):
    each = BLOCK * BLOCK // FETCHES
    copies = []
    for fetch in range(FETCHES):
        part = pl.ds(each * fetch, each)
        copies.append(
            pltpu.make_async_copy(rows_hbm.at[part], rows_ref.at[part], row_sem.at[fetch])
        )
        copies[fetch].start()
    table = pltpu.make_async_copy(dft_hbm, dft_ref, table_sem)
    table.start()
    down = lax.broadcasted_iota(jnp.int32, (FREQS, BLOCK), 0)
    across = lax.broadcasted_iota(jnp.int32, (FREQS, BLOCK), 1)
    bins = bin_of(down)
    for tile in range(FREQS // BLOCK):
        lanes = slice(tile * BLOCK, (tile + 1) * BLOCK)
        column = bin_of(across[:8] + tile * BLOCK)[:1]
        near = jnp.abs(bins - column) <= HALF
        band_ref[:, lanes] = jnp.where(near, 1.0, 0.0).astype(jnp.bfloat16)
        order_ref[:, lanes] = jnp.where(down == column, 1.0, 0.0).astype(jnp.bfloat16)

    def channel(chan, carry):
        x = []
        for pair in range(RADIX // 2):
            tile = rows_ref[pl.ds(pl.multiple_of(BLOCK * chan + 16 * pair, 16), 16), :]
            tile = tile.astype(jnp.float32)
            x += [tile[:8], tile[8:]]
        for unit, sums in enumerate(butterflies(x)):
            for side in range(2):
                sums_ref[2 * unit + side, pl.ds(pl.multiple_of(8 * chan, 8), 8), :] = sums[side]
        return carry

    for fetch in range(FETCHES):
        copies[fetch].wait()
        count = BLOCK // FETCHES
        lax.fori_loop(count * fetch, count * (fetch + 1), channel, 0, unroll=4)

    lane = lax.broadcasted_iota(jnp.int32, (1, BLOCK), 1)
    sign = jnp.where((lane < 32) | (lane >= 96), 1.0, -1.0)
    table.wait()
    found = []
    for unit in range(RADIX // 2):
        tiles = []
        for side in range(2):
            for seg in range(2):
                tiles.append(
                    jnp.concatenate(
                        [
                            sums_ref[2 * unit + side, pl.ds(2 * tile + seg, BLOCK, stride=8), :]
                            for tile in range(4)
                        ],
                        axis=1,
                    )
                )
        exact = jnp.concatenate(tiles, axis=0)
        high = exact.astype(jnp.bfloat16)
        low = (exact - high.astype(jnp.float32)).astype(jnp.bfloat16)
        first = jnp.dot(high, dft_ref[unit], preferred_element_type=jnp.float32)
        rest = jnp.dot(low, dft_ref[unit, :, :BLOCK], preferred_element_type=jnp.float32)
        both = first[:, :BLOCK] + (first[:, BLOCK:] + rest)
        one, two = both[: 2 * BLOCK], both[2 * BLOCK :]
        if unit == 0:
            found.append(jnp.where((lane >> 5) & 1 == 0, one, two))
        else:
            found.append(one + sign * pltpu.roll(two, 64, 1))
    left = lax.broadcasted_iota(jnp.int32, (2 * BLOCK, BLOCK), 1) < 64
    real = []
    imag = []
    for one, two in zip(found[0::2], found[1::2]):
        real.append(jnp.where(left, one, pltpu.roll(two, 64, 1)))
        imag.append(jnp.where(left, pltpu.roll(one, 64, 1), two))
    real = jnp.concatenate(real, axis=1)
    imag = jnp.concatenate(imag, axis=1)
    amplitude = jnp.sqrt(real * real + imag * imag)
    high = amplitude.astype(jnp.bfloat16)
    low = (amplitude - high.astype(jnp.float32)).astype(jnp.bfloat16)
    band = band_ref[...]
    total = jnp.dot(high, band, preferred_element_type=jnp.float32)
    total = total + jnp.dot(low, band, preferred_element_type=jnp.float32)
    count = jnp.dot(jnp.ones((8, FREQS), jnp.bfloat16), band, preferred_element_type=jnp.float32)
    divisor = jnp.maximum(total / count[:1], 1.0)
    for part, spectrum in enumerate([real, imag]):
        white = (spectrum / divisor).astype(jnp.bfloat16)
        turned = lax.dot_general(
            order_ref[...], white, (((1,), (1,)), ((), ())), preferred_element_type=jnp.float32
        )
        pieces = [
            turned[:, BLOCK * seg : BLOCK * (seg + 1)].reshape(FREQS // 8, 1, 8, BLOCK)
            for seg in range(2)
        ]
        both = jnp.concatenate(pieces, axis=1).reshape(NBLK, 2 * GROUP, BLOCK)
        out_ref[:, part * 2 * GROUP : (part + 1) * 2 * GROUP, :] = both.astype(jnp.bfloat16)


def select_kernel(first_ref, second_ref, place_ref, held_ref, out_ref, rows_ref):
    lane = lax.broadcasted_iota(jnp.int32, (32, BLOCK), 1)
    place = place_ref[0]
    left = (((lane >> 5) - place) & 3) < 2

    def turn(block, carry):
        tiles = held_ref[block].astype(jnp.float32)
        halves = [[tiles[0:16], tiles[32:48]], [tiles[16:32], tiles[48:64]]]
        for lead in range(2):
            order = halves[lead] + halves[1 - lead]
            rows_ref[lead, block] = jnp.concatenate(order + order, axis=0).T.astype(jnp.bfloat16)
        return carry

    lax.fori_loop(0, NBLK, turn, 0, unroll=8)

    def send(chan, carry):
        slots = [SLOT_DEV * chan + slot for slot in range(SLOT_DEV)]
        for seg in range(4):
            core = seg % 2
            dest = NBLK * seg + chan
            for slot in range(SLOT_DEV):
                second = second_ref[slots[slot]]
                for part in range(2):
                    out_ref[dest, pl.ds(32 * slot + 16 * part, 16), :] = held_ref[
                        second, pl.ds(32 * part + 16 * core, 16), :
                    ]
            lead = (place & 1) ^ core
            one = rows_ref[lead, first_ref[slots[0]], pl.ds(32 * seg, 32), :]
            two = rows_ref[lead, first_ref[slots[1]], pl.ds(32 * seg, 32), :]
            out_ref[dest, pl.ds(64, 32), :] = jnp.where(left, one, two)
        return carry

    lax.fori_loop(0, NBLK, send, 0, unroll=8)


def cross_of(slot, half, pair, second_ref, own_ref, mask):
    lane = lax.broadcasted_iota(jnp.int32, (32, BLOCK), 1) >> 5
    place = 2 * slot + half
    upper = []
    lower = []
    first = []
    for group in range(2):
        lanes = None
        for block in range(4):
            src = NBLK * ((block - place) % 4) + 2 * pair + group
            real = second_ref[src, pl.ds(32 * slot, 16), :]
            imag = second_ref[src, pl.ds(32 * slot + 16, 16), :]
            upper += [real, imag]
            lower += [-imag, real]
            piece = own_ref[src, pl.ds(64, 32), :]
            lanes = piece if lanes is None else jnp.where(lane == block, piece, lanes)
        first.append(lanes)
    second = jnp.concatenate(
        [jnp.concatenate(upper, axis=0), jnp.concatenate(lower, axis=0)], axis=1
    )
    first = jnp.concatenate(first, axis=1)
    spread = [jnp.broadcast_to(first[i : i + 1], (GROUP, 256)) * mask for i in range(32)]
    found = jnp.dot(
        jnp.concatenate(spread, axis=0), second, preferred_element_type=jnp.float32
    ).astype(jnp.bfloat16)
    return [
        found[:, part * BLOCK : (part + 1) * BLOCK].reshape(32, GROUP, BLOCK) for part in range(2)
    ]


def near_kernel(own_ref, mask_ref, cross_ref):
    for slot in range(SLOT_DEV):

        def cross(pair, carry):
            for part, found in enumerate(cross_of(slot, 0, pair, own_ref, own_ref, mask_ref[...])):
                cross_ref[slot, :, 2 * pair + part] = found
            return carry

        lax.fori_loop(0, NBLK // 2, cross, 0, unroll=UNROLL)


def correlate_kernel(
    core_ref, own_ref, other_ref, near_ref, mask_ref, table_ref, out_hbm, cross_ref, lag_ref, out_sem
):
    core = core_ref[0]
    leaving = []
    for slot in range(SLOT_DEV):

        def cross(pair, carry):
            for part, found in enumerate(
                cross_of(slot, 1, pair, other_ref, own_ref, mask_ref[...])
            ):
                cross_ref[:, 2 * pair + part] = found
            return carry

        def lags(pair, carry):
            sides = []
            for k in range(2):
                near = near_ref[slot, 2 * pair + k].reshape(FREQS, BLOCK)
                far = cross_ref[2 * pair + k].reshape(FREQS, BLOCK)
                sides.append(jnp.concatenate([near, far], axis=0))
            lagged = jnp.dot(
                table_ref[core], jnp.concatenate(sides, axis=1), preferred_element_type=jnp.float32
            )
            both = lagged.T
            for k in range(2):
                lag_ref[slot, 2 * pair + k] = both[k * BLOCK : (k + 1) * BLOCK]
            return carry

        lax.fori_loop(0, NBLK // 2, cross, 0, unroll=UNROLL)
        for step in range(16 // PAIRS):
            lax.fori_loop(PAIRS * step, PAIRS * (step + 1), lags, 0, unroll=True)
            rows = pl.ds(2 * PAIRS * step, 2 * PAIRS)
            copy = pltpu.make_async_copy(
                lag_ref.at[slot, rows], out_hbm.at[rows, slot], out_sem.at[slot, step]
            )
            copy.start()
            leaving.append(copy)
    for copy in leaving:
        copy.wait()


def front(traces):
    rows = traces.reshape(BLOCK, 2, SAMPLES // BLOCK, BLOCK).transpose(0, 2, 1, 3)
    rows = rows.reshape(BLOCK * BLOCK, BLOCK)
    return pl.pallas_call(
        front_kernel,
        out_shape=jax.ShapeDtypeStruct((NBLK, 4 * GROUP, BLOCK), jnp.bfloat16),
        in_specs=[pl.BlockSpec(memory_space=pltpu.HBM)] * 2,
        out_specs=pl.BlockSpec(memory_space=pltpu.VMEM),
        scratch_shapes=[
            pltpu.VMEM((BLOCK * BLOCK, BLOCK), jnp.bfloat16),
            pltpu.VMEM((RADIX // 2, SAMPLES // RADIX, 2 * BLOCK), jnp.bfloat16),
            pltpu.VMEM((FREQS, FREQS), jnp.bfloat16),
            pltpu.VMEM((FREQS, FREQS), jnp.bfloat16),
            pltpu.VMEM((RADIX, 8 * BLOCK, BLOCK), jnp.float32),
            pltpu.SemaphoreType.DMA((FETCHES,)),
            pltpu.SemaphoreType.DMA,
        ],
        compiler_params=pltpu.CompilerParams(vmem_limit_bytes=VMEM),
        name="front",
    )(
        pltpu.with_memory_space_constraint(rows, pltpu.HBM),
        pltpu.with_memory_space_constraint(jnp.asarray(dft_tables()), pltpu.HBM),
    )


def select(slot_first, slot_second, place, held):
    smem = pl.BlockSpec(memory_space=pltpu.SMEM)
    return pl.pallas_call(
        select_kernel,
        out_shape=jax.ShapeDtypeStruct((128, 96, BLOCK), jnp.bfloat16),
        in_specs=[smem, smem, smem, pl.BlockSpec(memory_space=pltpu.VMEM)],
        scratch_shapes=[pltpu.VMEM((2, NBLK, BLOCK, BLOCK), jnp.bfloat16)],
        compiler_params=pltpu.CompilerParams(vmem_limit_bytes=VMEM),
        name="select",
    )(slot_first, slot_second, place, held)


def near_cross(own):
    vmem = pl.BlockSpec(memory_space=pltpu.VMEM)
    return pl.pallas_call(
        near_kernel,
        out_shape=jax.ShapeDtypeStruct((SLOT_DEV, 32, NBLK, GROUP, BLOCK), jnp.bfloat16),
        in_specs=[vmem, vmem],
        out_specs=vmem,
        compiler_params=pltpu.CompilerParams(vmem_limit_bytes=16 * 1024 * 1024),
        cost_estimate=pl.CostEstimate(flops=8 << 30, transcendentals=0, bytes_accessed=11 << 20),
        name="near_cross",
    )(own, jnp.asarray(group_mask()))


def correlate(core, own, other, near=None):
    near = near_cross(own) if near is None else near
    vmem = pl.BlockSpec(memory_space=pltpu.VMEM)
    return pl.pallas_call(
        correlate_kernel,
        out_shape=jax.ShapeDtypeStruct((32, SLOT_DEV, BLOCK, LAGS), jnp.float32),
        in_specs=[pl.BlockSpec(memory_space=pltpu.SMEM)] + [vmem] * 5,
        out_specs=pl.BlockSpec(memory_space=pl.ANY),
        scratch_shapes=[
            pltpu.VMEM((32, NBLK, GROUP, BLOCK), jnp.bfloat16),
            pltpu.VMEM((SLOT_DEV, 32, BLOCK, LAGS), jnp.float32),
            pltpu.SemaphoreType.DMA((SLOT_DEV, 16 // PAIRS)),
        ],
        compiler_params=pltpu.CompilerParams(vmem_limit_bytes=24 * 1024 * 1024),
        name="correlate",
    )(core, own, other, near, jnp.asarray(group_mask()), jnp.asarray(lag_tables()))


def on_device(traces, pair_offsets, pair_counts, pair_owner):
    slot_first, slot_second = pair_blocks(
        pair_offsets, pair_counts, pair_owner, NBLK, SLOT_DEV * NBLK
    )
    seg = lax.axis_index("seg").astype(jnp.int32).reshape(1)
    held = lax.all_to_all(front(traces), "chan", split_axis=0, concat_axis=0, tiled=True)
    sent = select(slot_first, slot_second, seg, held)
    own = lax.all_to_all(sent, ("seg", "chan"), split_axis=0, concat_axis=0, tiled=True)
    other = lax.ppermute(own[:, :64], "seg", [(0, 1), (1, 0), (2, 3), (3, 2)])
    return correlate(seg % 2, own, other, near_cross(own))


def solution(mesh):
    placed = (P("chan", "seg", None), P(), P(), P())
    return jax.shard_map(
        on_device,
        mesh=mesh,
        in_specs=placed,
        out_specs=P("seg", "chan", None, None),
        check_vma=False,
    )
```

```python
import math

import jax
import jax.numpy as jnp
import ml_dtypes
import numpy as np
from jax import lax
from jax.experimental import pallas as pl
from jax.experimental.pallas import tpu as pltpu
from jax.sharding import PartitionSpec as P

SAMPLES = 8192
BAND_START = 32
FREQS = 512
HALF = 8
LAGS = 256
BLOCK = 128
NBLK = 32
SEGS = 8
SLOT_DEV = 2
GROUP = 16
RADIX = 16
VMEM = 32 * 1024 * 1024
PAIRS = 4
UNROLL = 16
FETCHES = 8


def bin_order():
    residues = [(0, 8)] + [(unit, RADIX - unit) for unit in range(1, RADIX // 2)]
    return (np.array(residues)[:, :, None] + RADIX * np.arange(FREQS // RADIX)).reshape(-1)


def dft_tables():
    run = SAMPLES // RADIX
    ring = 2.0 * math.pi / SAMPLES * np.arange(SAMPLES)
    bins = bin_order().reshape(RADIX // 2, 1, 2 * FREQS // RADIX)
    phase = np.arange(run)[None, :, None] * (BAND_START + bins) % SAMPLES
    table = np.concatenate([np.cos(ring)[phase], -np.sin(ring)[phase]], axis=2)
    high = table.astype(np.float32).astype(ml_dtypes.bfloat16)
    low = (table - high.astype(np.float64)).astype(np.float32).astype(ml_dtypes.bfloat16)
    return np.concatenate([high, low], axis=2)


def lag_tables():
    shifts = np.arange(LAGS // 2 + 8)
    phase = np.outer(BAND_START + np.arange(FREQS), shifts) % SAMPLES
    angles = phase.astype(np.float32) * np.float32(2.0 * math.pi / SAMPLES)
    norm = 1.0 / math.sqrt(FREQS * SEGS)
    parts = np.stack([np.cos(angles), -np.sin(angles)]).astype(ml_dtypes.bfloat16)
    parts = (parts.astype(np.float32) * norm).astype(ml_dtypes.bfloat16)
    parts = parts.reshape(2, NBLK // 2, 2, 2, GROUP // 2, LAGS // 2 + 8).transpose(0, 5, 3, 1, 2, 4)
    both = np.stack([parts, parts[:, :, ::-1]])
    return both.reshape(2, 2, LAGS // 2 + 8, FREQS)


def group_mask():
    lane, row = np.arange(256)[None, :], np.arange(GROUP)[:, None]
    same = (lane // 128 == row // 8) & (lane % 8 == row % 8)
    return same.astype(ml_dtypes.bfloat16)


def pair_blocks(pair_offsets, pair_counts, pair_owner, block_count, slot_count):
    slot_index = lax.iota(jnp.int32, slot_count)
    starts = jnp.cumsum(pair_counts) - pair_counts
    first_block = jnp.sum((starts[None, :] <= slot_index[:, None]).astype(jnp.int32), axis=1) - 1
    member = lax.iota(jnp.int32, block_count)[None, :] == first_block[:, None]
    start_of = jnp.sum(jnp.where(member, starts[None, :], 0), axis=1)
    position = slot_index - start_of
    listed = jnp.sum(jnp.where(member[:, :, None], pair_offsets[None, :, :], 0), axis=1)
    chosen = lax.iota(jnp.int32, pair_offsets.shape[1])[None, :] == position[:, None]
    offset = jnp.sum(jnp.where(chosen, listed, 0), axis=1)
    second_block = jnp.mod(first_block + offset, block_count)
    held = pair_owner[None, :] == slot_index[:, None]
    slot_first = jnp.sum(jnp.where(held, first_block[None, :], 0), axis=1)
    slot_second = jnp.sum(jnp.where(held, second_block[None, :], 0), axis=1)
    return (slot_first, slot_second)


def butterflies(x):
    root, c1, c3 = math.sqrt(0.5), math.cos(math.pi / 8), math.cos(3 * math.pi / 8)
    a = [x[n] + x[n + 8] for n in range(8)]
    b = [x[n] - x[n + 8] for n in range(8)]
    c = [a[n] + a[n + 4] for n in range(4)]
    d = [a[n] - a[n + 4] for n in range(4)]
    even, odd = c[0] + c[2], c[1] + c[3]
    g, h = (d[1] - d[3]) * root, (d[1] + d[3]) * root
    p = [None] + [b[n] - b[8 - n] for n in range(1, 4)]
    q = [None] + [b[n] + b[8 - n] for n in range(1, 4)]
    p2, q2 = p[2] * root, q[2] * root
    re1, re3 = p[1] * c1 + p[3] * c3, p[1] * c3 - p[3] * c1
    im1, im3 = q[1] * c3 + q[3] * c1, q[1] * c1 - q[3] * c3
    plus, minus = b[0] + p2, b[0] - p2
    over, under = q2 + b[4], q2 - b[4]
    return [
        (even + odd, even - odd),
        (plus + re1, im1 + over),
        (d[0] + g, d[2] + h),
        (minus + re3, im3 + under),
        (c[0] - c[2], c[1] - c[3]),
        (minus - re3, im3 - under),
        (d[0] - g, h - d[2]),
        (plus - re1, im1 - over),
    ]


def bin_of(column):
    unit, side, group = column >> 6, (column >> 5) & 1, column & 31
    other = jnp.where(unit == 0, RADIX // 2, RADIX - unit)
    return RADIX * group + jnp.where(side == 0, unit, other)


def front_kernel(
    rows_hbm, dft_hbm, out_ref, rows_ref, dft_ref, band_ref, order_ref, sums_ref, row_sem, table_sem
):
    each = BLOCK * BLOCK // FETCHES
    copies = []
    for fetch in range(FETCHES):
        part = pl.ds(each * fetch, each)
        copies.append(
            pltpu.make_async_copy(rows_hbm.at[part], rows_ref.at[part], row_sem.at[fetch])
        )
        copies[fetch].start()
    table = pltpu.make_async_copy(dft_hbm, dft_ref, table_sem)
    table.start()
    down = lax.broadcasted_iota(jnp.int32, (FREQS, BLOCK), 0)
    across = lax.broadcasted_iota(jnp.int32, (FREQS, BLOCK), 1)
    bins = bin_of(down)
    for tile in range(FREQS // BLOCK):
        lanes = slice(tile * BLOCK, (tile + 1) * BLOCK)
        column = bin_of(across[:8] + tile * BLOCK)[:1]
        near = jnp.abs(bins - column) <= HALF
        band_ref[:, lanes] = jnp.where(near, 1.0, 0.0).astype(jnp.bfloat16)
        order_ref[:, lanes] = jnp.where(down == column, 1.0, 0.0).astype(jnp.bfloat16)

    def channel(chan, carry):
        x = []
        for pair in range(RADIX // 2):
            tile = rows_ref[pl.ds(pl.multiple_of(BLOCK * chan + 16 * pair, 16), 16), :]
            tile = tile.astype(jnp.float32)
            x += [tile[:8], tile[8:]]
        for unit, sums in enumerate(butterflies(x)):
            for side in range(2):
                sums_ref[2 * unit + side, pl.ds(pl.multiple_of(8 * chan, 8), 8), :] = sums[side]
        return carry

    for fetch in range(FETCHES):
        copies[fetch].wait()
        count = BLOCK // FETCHES
        lax.fori_loop(count * fetch, count * (fetch + 1), channel, 0, unroll=4)

    lane = lax.broadcasted_iota(jnp.int32, (1, BLOCK), 1)
    sign = jnp.where((lane < 32) | (lane >= 96), 1.0, -1.0)
    table.wait()
    found = []
    for unit in range(RADIX // 2):
        tiles = []
        for side in range(2):
            for seg in range(2):
                tiles.append(
                    jnp.concatenate(
                        [
                            sums_ref[2 * unit + side, pl.ds(2 * tile + seg, BLOCK, stride=8), :]
                            for tile in range(4)
                        ],
                        axis=1,
                    )
                )
        exact = jnp.concatenate(tiles, axis=0)
        high = exact.astype(jnp.bfloat16)
        low = (exact - high.astype(jnp.float32)).astype(jnp.bfloat16)
        first = jnp.dot(high, dft_ref[unit], preferred_element_type=jnp.float32)
        rest = jnp.dot(low, dft_ref[unit, :, :BLOCK], preferred_element_type=jnp.float32)
        both = first[:, :BLOCK] + (first[:, BLOCK:] + rest)
        one, two = both[: 2 * BLOCK], both[2 * BLOCK :]
        if unit == 0:
            found.append(jnp.where((lane >> 5) & 1 == 0, one, two))
        else:
            found.append(one + sign * pltpu.roll(two, 64, 1))
    left = lax.broadcasted_iota(jnp.int32, (2 * BLOCK, BLOCK), 1) < 64
    real = []
    imag = []
    for one, two in zip(found[0::2], found[1::2]):
        real.append(jnp.where(left, one, pltpu.roll(two, 64, 1)))
        imag.append(jnp.where(left, pltpu.roll(one, 64, 1), two))
    real = jnp.concatenate(real, axis=1)
    imag = jnp.concatenate(imag, axis=1)
    amplitude = jnp.sqrt(real * real + imag * imag)
    high = amplitude.astype(jnp.bfloat16)
    low = (amplitude - high.astype(jnp.float32)).astype(jnp.bfloat16)
    band = band_ref[...]
    total = jnp.dot(high, band, preferred_element_type=jnp.float32)
    total = total + jnp.dot(low, band, preferred_element_type=jnp.float32)
    count = jnp.dot(jnp.ones((8, FREQS), jnp.bfloat16), band, preferred_element_type=jnp.float32)
    divisor = jnp.maximum(total / count[:1], 1.0)
    for part, spectrum in enumerate([real, imag]):
        white = (spectrum / divisor).astype(jnp.bfloat16)
        turned = lax.dot_general(
            order_ref[...], white, (((1,), (1,)), ((), ())), preferred_element_type=jnp.float32
        )
        pieces = [
            turned[:, BLOCK * seg : BLOCK * (seg + 1)].reshape(FREQS // 8, 1, 8, BLOCK)
            for seg in range(2)
        ]
        both = jnp.concatenate(pieces, axis=1).reshape(NBLK, 2 * GROUP, BLOCK)
        out_ref[:, part * 2 * GROUP : (part + 1) * 2 * GROUP, :] = both.astype(jnp.bfloat16)


def select_kernel(first_ref, second_ref, place_ref, held_ref, out_ref, rows_ref):
    lane = lax.broadcasted_iota(jnp.int32, (32, BLOCK), 1)
    place = place_ref[0]
    left = (((lane >> 5) - place) & 3) < 2

    def turn(block, carry):
        tiles = held_ref[block].astype(jnp.float32)
        halves = [[tiles[0:16], tiles[32:48]], [tiles[16:32], tiles[48:64]]]
        for lead in range(2):
            order = halves[lead] + halves[1 - lead]
            rows_ref[lead, block] = jnp.concatenate(order + order, axis=0).T.astype(jnp.bfloat16)
        return carry

    lax.fori_loop(0, NBLK, turn, 0, unroll=8)

    def send(chan, carry):
        slots = [SLOT_DEV * chan + slot for slot in range(SLOT_DEV)]
        for seg in range(4):
            core = seg % 2
            dest = NBLK * seg + chan
            for slot in range(SLOT_DEV):
                second = second_ref[slots[slot]]
                for part in range(2):
                    out_ref[dest, pl.ds(32 * slot + 16 * part, 16), :] = held_ref[
                        second, pl.ds(32 * part + 16 * core, 16), :
                    ]
            lead = (place & 1) ^ core
            one = rows_ref[lead, first_ref[slots[0]], pl.ds(32 * seg, 32), :]
            two = rows_ref[lead, first_ref[slots[1]], pl.ds(32 * seg, 32), :]
            out_ref[dest, pl.ds(64, 32), :] = jnp.where(left, one, two)
        return carry

    lax.fori_loop(0, NBLK, send, 0, unroll=8)


def cross_of(slot, half, pair, second_ref, own_ref, mask):
    lane = lax.broadcasted_iota(jnp.int32, (32, BLOCK), 1) >> 5
    place = 2 * slot + half
    upper = []
    lower = []
    first = []
    for group in range(2):
        lanes = None
        for block in range(4):
            src = NBLK * ((block - place) % 4) + 2 * pair + group
            real = second_ref[src, pl.ds(32 * slot, 16), :]
            imag = second_ref[src, pl.ds(32 * slot + 16, 16), :]
            upper += [real, imag]
            lower += [-imag, real]
            piece = own_ref[src, pl.ds(64, 32), :]
            lanes = piece if lanes is None else jnp.where(lane == block, piece, lanes)
        first.append(lanes)
    second = jnp.concatenate(
        [jnp.concatenate(upper, axis=0), jnp.concatenate(lower, axis=0)], axis=1
    )
    first = jnp.concatenate(first, axis=1)
    spread = [jnp.broadcast_to(first[i : i + 1], (GROUP, 256)) * mask for i in range(32)]
    found = jnp.dot(
        jnp.concatenate(spread, axis=0), second, preferred_element_type=jnp.float32
    ).astype(jnp.bfloat16)
    return [
        found[:, part * BLOCK : (part + 1) * BLOCK].reshape(32, GROUP, BLOCK) for part in range(2)
    ]


def near_kernel(own_ref, mask_ref, cross_ref):
    for slot in range(SLOT_DEV):

        def cross(pair, carry):
            for part, found in enumerate(cross_of(slot, 0, pair, own_ref, own_ref, mask_ref[...])):
                cross_ref[slot, :, NBLK // 2 * part + pair] = found
            return carry

        lax.fori_loop(0, NBLK // 2, cross, 0, unroll=UNROLL)


def correlate_kernel(
    core_ref, own_ref, other_ref, near_ref, mask_ref, table_ref, out_hbm, cross_ref, lag_ref, out_sem
):
    core = core_ref[0]
    leaving = []
    for slot in range(SLOT_DEV):

        def cross(pair, carry):
            for part, found in enumerate(
                cross_of(slot, 1, pair, other_ref, own_ref, mask_ref[...])
            ):
                cross_ref[:, NBLK // 2 * part + pair] = found
            return carry

        def lags(pair, carry):
            sums = []
            for part in range(2):
                tiles = pl.ds(NBLK // 2 * part, NBLK // 2)
                sides = []
                for k in range(2):
                    near = near_ref[slot, 2 * pair + k, tiles].reshape(FREQS // 2, BLOCK)
                    far = cross_ref[2 * pair + k, tiles].reshape(FREQS // 2, BLOCK)
                    sides.append(jnp.concatenate([near, far], axis=0))
                sums.append(
                    jnp.dot(
                        table_ref[core, part],
                        jnp.concatenate(sides, axis=1),
                        preferred_element_type=jnp.float32,
                    )
                )
            later = (sums[0][:BLOCK] + sums[1][:BLOCK]).T
            less = sums[0] - sums[1]
            row = lax.broadcasted_iota(jnp.int32, (8, 2 * BLOCK), 0)
            back = (8 - row) & 7
            turned = []
            for tile in range(15, -1, -1):
                here, above = less[8 * tile : 8 * tile + 8], less[8 * tile + 8 : 8 * tile + 16]
                turned.append(
                    jnp.take_along_axis(
                        jnp.where(row == 0, above, here), back, axis=0, mode="promise_in_bounds"
                    )
                )
            earlier = jnp.concatenate(turned, axis=0).T
            for k in range(2):
                rows = slice(k * BLOCK, (k + 1) * BLOCK)
                lag_ref[slot, 2 * pair + k, :, :BLOCK] = earlier[rows]
                lag_ref[slot, 2 * pair + k, :, BLOCK:] = later[rows]
            return carry

        lax.fori_loop(0, NBLK // 2, cross, 0, unroll=UNROLL)
        for step in range(16 // PAIRS):
            lax.fori_loop(PAIRS * step, PAIRS * (step + 1), lags, 0, unroll=True)
            rows = pl.ds(2 * PAIRS * step, 2 * PAIRS)
            copy = pltpu.make_async_copy(
                lag_ref.at[slot, rows], out_hbm.at[rows, slot], out_sem.at[slot, step]
            )
            copy.start()
            leaving.append(copy)
    for copy in leaving:
        copy.wait()


def front(traces):
    rows = traces.reshape(BLOCK, 2, SAMPLES // BLOCK, BLOCK).transpose(0, 2, 1, 3)
    rows = rows.reshape(BLOCK * BLOCK, BLOCK)
    return pl.pallas_call(
        front_kernel,
        out_shape=jax.ShapeDtypeStruct((NBLK, 4 * GROUP, BLOCK), jnp.bfloat16),
        in_specs=[pl.BlockSpec(memory_space=pltpu.HBM)] * 2,
        out_specs=pl.BlockSpec(memory_space=pltpu.VMEM),
        scratch_shapes=[
            pltpu.VMEM((BLOCK * BLOCK, BLOCK), jnp.bfloat16),
            pltpu.VMEM((RADIX // 2, SAMPLES // RADIX, 2 * BLOCK), jnp.bfloat16),
            pltpu.VMEM((FREQS, FREQS), jnp.bfloat16),
            pltpu.VMEM((FREQS, FREQS), jnp.bfloat16),
            pltpu.VMEM((RADIX, 8 * BLOCK, BLOCK), jnp.float32),
            pltpu.SemaphoreType.DMA((FETCHES,)),
            pltpu.SemaphoreType.DMA,
        ],
        compiler_params=pltpu.CompilerParams(vmem_limit_bytes=VMEM),
        name="front",
    )(
        pltpu.with_memory_space_constraint(rows, pltpu.HBM),
        pltpu.with_memory_space_constraint(jnp.asarray(dft_tables()), pltpu.HBM),
    )


def select(slot_first, slot_second, place, held):
    smem = pl.BlockSpec(memory_space=pltpu.SMEM)
    return pl.pallas_call(
        select_kernel,
        out_shape=jax.ShapeDtypeStruct((128, 96, BLOCK), jnp.bfloat16),
        in_specs=[smem, smem, smem, pl.BlockSpec(memory_space=pltpu.VMEM)],
        scratch_shapes=[pltpu.VMEM((2, NBLK, BLOCK, BLOCK), jnp.bfloat16)],
        compiler_params=pltpu.CompilerParams(vmem_limit_bytes=VMEM),
        name="select",
    )(slot_first, slot_second, place, held)


def near_cross(own):
    vmem = pl.BlockSpec(memory_space=pltpu.VMEM)
    return pl.pallas_call(
        near_kernel,
        out_shape=jax.ShapeDtypeStruct((SLOT_DEV, 32, NBLK, GROUP, BLOCK), jnp.bfloat16),
        in_specs=[vmem, vmem],
        out_specs=vmem,
        compiler_params=pltpu.CompilerParams(vmem_limit_bytes=16 * 1024 * 1024),
        cost_estimate=pl.CostEstimate(flops=8 << 30, transcendentals=0, bytes_accessed=11 << 20),
        name="near_cross",
    )(own, jnp.asarray(group_mask()))


def correlate(core, own, other, near=None):
    near = near_cross(own) if near is None else near
    vmem = pl.BlockSpec(memory_space=pltpu.VMEM)
    return pl.pallas_call(
        correlate_kernel,
        out_shape=jax.ShapeDtypeStruct((32, SLOT_DEV, BLOCK, LAGS), jnp.float32),
        in_specs=[pl.BlockSpec(memory_space=pltpu.SMEM)] + [vmem] * 5,
        out_specs=pl.BlockSpec(memory_space=pl.ANY),
        scratch_shapes=[
            pltpu.VMEM((32, NBLK, GROUP, BLOCK), jnp.bfloat16),
            pltpu.VMEM((SLOT_DEV, 32, BLOCK, LAGS), jnp.float32),
            pltpu.SemaphoreType.DMA((SLOT_DEV, 16 // PAIRS)),
        ],
        compiler_params=pltpu.CompilerParams(vmem_limit_bytes=24 * 1024 * 1024),
        name="correlate",
    )(core, own, other, near, jnp.asarray(group_mask()), jnp.asarray(lag_tables()))


def on_device(traces, pair_offsets, pair_counts, pair_owner):
    slot_first, slot_second = pair_blocks(
        pair_offsets, pair_counts, pair_owner, NBLK, SLOT_DEV * NBLK
    )
    seg = lax.axis_index("seg").astype(jnp.int32).reshape(1)
    held = lax.all_to_all(front(traces), "chan", split_axis=0, concat_axis=0, tiled=True)
    sent = select(slot_first, slot_second, seg, held)
    own = lax.all_to_all(sent, ("seg", "chan"), split_axis=0, concat_axis=0, tiled=True)
    other = lax.ppermute(own[:, :64], "seg", [(0, 1), (1, 0), (2, 3), (3, 2)])
    return correlate(seg % 2, own, other, near_cross(own))


def solution(mesh):
    placed = (P("chan", "seg", None), P(), P(), P())
    return jax.shard_map(
        on_device,
        mesh=mesh,
        in_specs=placed,
        out_specs=P("seg", "chan", None, None),
        check_vma=False,
    )
```

```python
import math

import jax
import jax.numpy as jnp
import ml_dtypes
import numpy as np
from jax import lax
from jax.experimental import pallas as pl
from jax.experimental.pallas import tpu as pltpu
from jax.sharding import PartitionSpec as P

SAMPLES = 8192
BAND_START = 32
FREQS = 512
HALF = 8
LAGS = 256
BLOCK = 128
NBLK = 32
SEGS = 8
SLOT_DEV = 2
GROUP = 16
RADIX = 16
VMEM = 32 * 1024 * 1024
PAIRS = 4
UNROLL = 32
FETCHES = 8


def bin_order():
    residues = [(0, 8)] + [(unit, RADIX - unit) for unit in range(1, RADIX // 2)]
    return (np.array(residues)[:, :, None] + RADIX * np.arange(FREQS // RADIX)).reshape(-1)


def dft_tables():
    run = SAMPLES // RADIX
    ring = 2.0 * math.pi / SAMPLES * np.arange(SAMPLES)
    bins = bin_order().reshape(RADIX // 2, 1, 2 * FREQS // RADIX)
    phase = np.arange(run)[None, :, None] * (BAND_START + bins) % SAMPLES
    table = np.concatenate([np.cos(ring)[phase], -np.sin(ring)[phase]], axis=2)
    high = table.astype(np.float32).astype(ml_dtypes.bfloat16)
    low = (table - high.astype(np.float64)).astype(np.float32).astype(ml_dtypes.bfloat16)
    return np.concatenate([high, low], axis=2)


def lag_tables():
    shifts = np.arange(LAGS // 2 + 8)
    phase = np.outer(BAND_START + np.arange(FREQS), shifts) % SAMPLES
    angles = phase.astype(np.float32) * np.float32(2.0 * math.pi / SAMPLES)
    norm = 1.0 / math.sqrt(FREQS * SEGS)
    parts = np.stack([np.cos(angles), -np.sin(angles)]).astype(ml_dtypes.bfloat16)
    parts = (parts.astype(np.float32) * norm).astype(ml_dtypes.bfloat16)
    return parts.transpose(0, 2, 1)


def group_mask():
    lane, row = np.arange(256)[None, :], np.arange(GROUP)[:, None]
    return (lane // 16 % 2 * 8 + lane % 8 == row).astype(ml_dtypes.bfloat16)


def pair_blocks(pair_offsets, pair_counts, pair_owner, block_count, slot_count):
    slot_index = lax.iota(jnp.int32, slot_count)
    starts = jnp.cumsum(pair_counts) - pair_counts
    first_block = jnp.sum((starts[None, :] <= slot_index[:, None]).astype(jnp.int32), axis=1) - 1
    member = lax.iota(jnp.int32, block_count)[None, :] == first_block[:, None]
    start_of = jnp.sum(jnp.where(member, starts[None, :], 0), axis=1)
    position = slot_index - start_of
    listed = jnp.sum(jnp.where(member[:, :, None], pair_offsets[None, :, :], 0), axis=1)
    chosen = lax.iota(jnp.int32, pair_offsets.shape[1])[None, :] == position[:, None]
    offset = jnp.sum(jnp.where(chosen, listed, 0), axis=1)
    second_block = jnp.mod(first_block + offset, block_count)
    held = pair_owner[None, :] == slot_index[:, None]
    slot_first = jnp.sum(jnp.where(held, first_block[None, :], 0), axis=1)
    slot_second = jnp.sum(jnp.where(held, second_block[None, :], 0), axis=1)
    return (slot_first, slot_second)


def butterflies(x):
    root, c1, c3 = math.sqrt(0.5), math.cos(math.pi / 8), math.cos(3 * math.pi / 8)
    a = [x[n] + x[n + 8] for n in range(8)]
    b = [x[n] - x[n + 8] for n in range(8)]
    c = [a[n] + a[n + 4] for n in range(4)]
    d = [a[n] - a[n + 4] for n in range(4)]
    even, odd = c[0] + c[2], c[1] + c[3]
    g, h = (d[1] - d[3]) * root, (d[1] + d[3]) * root
    p = [None] + [b[n] - b[8 - n] for n in range(1, 4)]
    q = [None] + [b[n] + b[8 - n] for n in range(1, 4)]
    p2, q2 = p[2] * root, q[2] * root
    re1, re3 = p[1] * c1 + p[3] * c3, p[1] * c3 - p[3] * c1
    im1, im3 = q[1] * c3 + q[3] * c1, q[1] * c1 - q[3] * c3
    plus, minus = b[0] + p2, b[0] - p2
    over, under = q2 + b[4], q2 - b[4]
    return [
        (even + odd, even - odd),
        (plus + re1, im1 + over),
        (d[0] + g, d[2] + h),
        (minus + re3, im3 + under),
        (c[0] - c[2], c[1] - c[3]),
        (minus - re3, im3 - under),
        (d[0] - g, h - d[2]),
        (plus - re1, im1 - over),
    ]


def bin_of(column):
    unit, side, group = column >> 6, (column >> 5) & 1, column & 31
    other = jnp.where(unit == 0, RADIX // 2, RADIX - unit)
    return RADIX * group + jnp.where(side == 0, unit, other)


def front_kernel(
    rows_hbm, dft_hbm, out_ref, rows_ref, dft_ref, band_ref, order_ref, sums_ref, row_sem, table_sem
):
    each = BLOCK * BLOCK // FETCHES
    copies = []
    for fetch in range(FETCHES):
        part = pl.ds(each * fetch, each)
        copies.append(
            pltpu.make_async_copy(rows_hbm.at[part], rows_ref.at[part], row_sem.at[fetch])
        )
        copies[fetch].start()
    table = pltpu.make_async_copy(dft_hbm, dft_ref, table_sem)
    table.start()
    down = lax.broadcasted_iota(jnp.int32, (FREQS, BLOCK), 0)
    across = lax.broadcasted_iota(jnp.int32, (FREQS, BLOCK), 1)
    bins = bin_of(down)
    for tile in range(FREQS // BLOCK):
        lanes = slice(tile * BLOCK, (tile + 1) * BLOCK)
        column = bin_of(across[:8] + tile * BLOCK)[:1]
        near = jnp.abs(bins - column) <= HALF
        band_ref[:, lanes] = jnp.where(near, 1.0, 0.0).astype(jnp.bfloat16)
        order_ref[:, lanes] = jnp.where(down == column, 1.0, 0.0).astype(jnp.bfloat16)

    def channel(chan, carry):
        x = []
        for pair in range(RADIX // 2):
            tile = rows_ref[pl.ds(pl.multiple_of(BLOCK * chan + 16 * pair, 16), 16), :]
            tile = tile.astype(jnp.float32)
            x += [tile[:8], tile[8:]]
        for unit, sums in enumerate(butterflies(x)):
            for side in range(2):
                sums_ref[2 * unit + side, pl.ds(pl.multiple_of(8 * chan, 8), 8), :] = sums[side]
        return carry

    for fetch in range(FETCHES):
        copies[fetch].wait()
        count = BLOCK // FETCHES
        lax.fori_loop(count * fetch, count * (fetch + 1), channel, 0, unroll=4)

    lane = lax.broadcasted_iota(jnp.int32, (1, BLOCK), 1)
    sign = jnp.where((lane < 32) | (lane >= 96), 1.0, -1.0)
    table.wait()
    found = []
    for unit in range(RADIX // 2):
        tiles = []
        for side in range(2):
            for seg in range(2):
                tiles.append(
                    jnp.concatenate(
                        [
                            sums_ref[2 * unit + side, pl.ds(2 * tile + seg, BLOCK, stride=8), :]
                            for tile in range(4)
                        ],
                        axis=1,
                    )
                )
        exact = jnp.concatenate(tiles, axis=0)
        high = exact.astype(jnp.bfloat16)
        low = (exact - high.astype(jnp.float32)).astype(jnp.bfloat16)
        first = jnp.dot(high, dft_ref[unit], preferred_element_type=jnp.float32)
        rest = jnp.dot(low, dft_ref[unit, :, :BLOCK], preferred_element_type=jnp.float32)
        both = first[:, :BLOCK] + (first[:, BLOCK:] + rest)
        one, two = both[: 2 * BLOCK], both[2 * BLOCK :]
        if unit == 0:
            found.append(jnp.where((lane >> 5) & 1 == 0, one, two))
        else:
            found.append(one + sign * pltpu.roll(two, 64, 1))
    left = lax.broadcasted_iota(jnp.int32, (2 * BLOCK, BLOCK), 1) < 64
    real = []
    imag = []
    for one, two in zip(found[0::2], found[1::2]):
        real.append(jnp.where(left, one, pltpu.roll(two, 64, 1)))
        imag.append(jnp.where(left, pltpu.roll(one, 64, 1), two))
    real = jnp.concatenate(real, axis=1)
    imag = jnp.concatenate(imag, axis=1)
    amplitude = jnp.sqrt(real * real + imag * imag)
    high = amplitude.astype(jnp.bfloat16)
    low = (amplitude - high.astype(jnp.float32)).astype(jnp.bfloat16)
    band = band_ref[...]
    total = jnp.dot(high, band, preferred_element_type=jnp.float32)
    total = total + jnp.dot(low, band, preferred_element_type=jnp.float32)
    count = jnp.dot(jnp.ones((8, FREQS), jnp.bfloat16), band, preferred_element_type=jnp.float32)
    divisor = jnp.maximum(total / count[:1], 1.0)
    for part, spectrum in enumerate([real, imag]):
        white = (spectrum / divisor).astype(jnp.bfloat16)
        turned = lax.dot_general(
            order_ref[...], white, (((1,), (1,)), ((), ())), preferred_element_type=jnp.float32
        )
        pieces = [
            turned[:, BLOCK * seg : BLOCK * (seg + 1)].reshape(FREQS // 8, 1, 8, BLOCK)
            for seg in range(2)
        ]
        both = jnp.concatenate(pieces, axis=1).reshape(NBLK, 2 * GROUP, BLOCK)
        out_ref[:, part * 2 * GROUP : (part + 1) * 2 * GROUP, :] = both.astype(jnp.bfloat16)


def select_kernel(first_ref, second_ref, place_ref, held_ref, out_ref, rows_ref):
    lane = lax.broadcasted_iota(jnp.int32, (32, BLOCK), 1)
    left = (lane < 64) == ((place_ref[0] & 1) == 0)

    def turn(block, carry):
        tiles = held_ref[block].astype(jnp.float32)
        rows_ref[block] = jnp.concatenate([tiles, tiles], axis=0).T.astype(jnp.bfloat16)
        return carry

    lax.fori_loop(0, NBLK, turn, 0, unroll=True)

    def send(chan, carry):
        slots = [SLOT_DEV * chan + slot for slot in range(SLOT_DEV)]
        for seg in range(4):
            dest = NBLK * seg + chan
            out_ref[dest, pl.ds(0, 64), :] = held_ref[second_ref[slots[seg % 2]]]
            one = rows_ref[first_ref[slots[0]], pl.ds(32 * seg, 32), :]
            two = rows_ref[first_ref[slots[1]], pl.ds(32 * seg, 32), :]
            out_ref[dest, pl.ds(64, 32), :] = jnp.where(left, one, two)
        return carry

    lax.fori_loop(0, NBLK, send, 0, unroll=True)


def correlate_kernel(
    slot_ref, second_ref, own_ref, mask_ref, table_ref, filled_hbm, out_hbm, cross_ref, lag_ref, out_sem
):
    del filled_hbm
    slot = slot_ref[0]

    def cross(group, carry):
        left = lax.broadcasted_iota(jnp.int32, (32, BLOCK), 1) < 64
        upper = []
        lower = []
        lanes = []
        for seg in range(4):
            src = NBLK * (seg ^ slot) + group
            real, imag = second_ref[src, pl.ds(0, 32), :], second_ref[src, pl.ds(32, 32), :]
            upper += [real, imag]
            lower += [-imag, real]
            lanes.append(own_ref[src, pl.ds(64, 32), :])
        second = jnp.concatenate(
            [jnp.concatenate(upper, axis=0), jnp.concatenate(lower, axis=0)], axis=1
        )
        first = jnp.concatenate(
            [jnp.where(left, lanes[0], lanes[1]), jnp.where(left, lanes[2], lanes[3])], axis=1
        )
        mask = mask_ref[...]
        spread = [jnp.broadcast_to(first[i : i + 1], (GROUP, 256)) * mask for i in range(32)]
        found = jnp.dot(
            jnp.concatenate(spread, axis=0), second, preferred_element_type=jnp.float32
        ).astype(jnp.bfloat16)
        for part in range(2):
            cross_ref[:, NBLK * part + group] = found[:, part * BLOCK : (part + 1) * BLOCK].reshape(
                32, GROUP, BLOCK
            )
        return carry

    def lags(pair, carry):
        sums = []
        for part in range(2):
            tiles = pl.ds(NBLK * part, NBLK)
            sides = [cross_ref[2 * pair + k, tiles].reshape(FREQS, BLOCK) for k in range(2)]
            sums.append(
                jnp.dot(
                    table_ref[part],
                    jnp.concatenate(sides, axis=1),
                    preferred_element_type=jnp.float32,
                )
            )
        later = (sums[0][:BLOCK] + sums[1][:BLOCK]).T
        less = sums[0] - sums[1]
        row = lax.broadcasted_iota(jnp.int32, (8, 2 * BLOCK), 0)
        back = (8 - row) & 7
        turned = []
        for tile in range(15, -1, -1):
            here, above = less[8 * tile : 8 * tile + 8], less[8 * tile + 8 : 8 * tile + 16]
            turned.append(
                jnp.take_along_axis(
                    jnp.where(row == 0, above, here), back, axis=0, mode="promise_in_bounds"
                )
            )
        earlier = jnp.concatenate(turned, axis=0).T
        for k in range(2):
            rows = slice(k * BLOCK, (k + 1) * BLOCK)
            lag_ref[2 * pair + k, :, :BLOCK] = earlier[rows]
            lag_ref[2 * pair + k, :, BLOCK:] = later[rows]
        return carry

    leaving = []
    lax.fori_loop(0, NBLK, cross, 0, unroll=UNROLL)
    for step in range(16 // PAIRS):
        lax.fori_loop(PAIRS * step, PAIRS * (step + 1), lags, 0, unroll=True)
        rows = pl.ds(2 * PAIRS * step, 2 * PAIRS)
        copy = pltpu.make_async_copy(lag_ref.at[rows], out_hbm.at[rows, slot], out_sem.at[step])
        copy.start()
        leaving.append(copy)
    for copy in leaving:
        copy.wait()


def front(traces):
    rows = traces.reshape(BLOCK, 2, SAMPLES // BLOCK, BLOCK).transpose(0, 2, 1, 3)
    rows = rows.reshape(BLOCK * BLOCK, BLOCK)
    return pl.pallas_call(
        front_kernel,
        out_shape=jax.ShapeDtypeStruct((NBLK, 4 * GROUP, BLOCK), jnp.bfloat16),
        in_specs=[pl.BlockSpec(memory_space=pltpu.HBM)] * 2,
        out_specs=pl.BlockSpec(memory_space=pltpu.VMEM),
        scratch_shapes=[
            pltpu.VMEM((BLOCK * BLOCK, BLOCK), jnp.bfloat16),
            pltpu.VMEM((RADIX // 2, SAMPLES // RADIX, 2 * BLOCK), jnp.bfloat16),
            pltpu.VMEM((FREQS, FREQS), jnp.bfloat16),
            pltpu.VMEM((FREQS, FREQS), jnp.bfloat16),
            pltpu.VMEM((RADIX, 8 * BLOCK, BLOCK), jnp.float32),
            pltpu.SemaphoreType.DMA((FETCHES,)),
            pltpu.SemaphoreType.DMA,
        ],
        compiler_params=pltpu.CompilerParams(vmem_limit_bytes=VMEM),
        name="front",
    )(
        pltpu.with_memory_space_constraint(rows, pltpu.HBM),
        pltpu.with_memory_space_constraint(jnp.asarray(dft_tables()), pltpu.HBM),
    )


def select(slot_first, slot_second, place, held):
    smem = pl.BlockSpec(memory_space=pltpu.SMEM)
    return pl.pallas_call(
        select_kernel,
        out_shape=jax.ShapeDtypeStruct((128, 96, BLOCK), jnp.bfloat16),
        in_specs=[smem, smem, smem, pl.BlockSpec(memory_space=pltpu.VMEM)],
        scratch_shapes=[pltpu.VMEM((NBLK, BLOCK, BLOCK), jnp.bfloat16)],
        compiler_params=pltpu.CompilerParams(vmem_limit_bytes=VMEM),
        name="select",
    )(slot_first, slot_second, place, held)


def correlate_slot(slot, second, own, filled=None):
    hbm = pl.BlockSpec(memory_space=pl.ANY)
    vmem = pl.BlockSpec(memory_space=pltpu.VMEM)
    kernel = correlate_kernel
    operands = [slot, second, own, jnp.asarray(group_mask()), jnp.asarray(lag_tables())]
    specs = [pl.BlockSpec(memory_space=pltpu.SMEM)] + [vmem] * 4
    aliases = {}
    if filled is None:
        kernel = lambda *refs: correlate_kernel(*refs[:5], None, *refs[5:])
    else:
        operands.append(filled)
        specs.append(hbm)
        aliases = {5: 0}
    return pl.pallas_call(
        kernel,
        out_shape=jax.ShapeDtypeStruct((32, SLOT_DEV, BLOCK, LAGS), jnp.float32),
        in_specs=specs,
        out_specs=hbm,
        scratch_shapes=[
            pltpu.VMEM((32, 2 * NBLK, GROUP, BLOCK), jnp.bfloat16),
            pltpu.VMEM((32, BLOCK, LAGS), jnp.float32),
            pltpu.SemaphoreType.DMA((16 // PAIRS,)),
        ],
        input_output_aliases=aliases,
        compiler_params=pltpu.CompilerParams(vmem_limit_bytes=24 * 1024 * 1024),
        cost_estimate=pl.CostEstimate(flops=8 << 30, transcendentals=0, bytes_accessed=9 << 20),
        name="correlate_first" if filled is None else "correlate_second",
    )(*operands)


def correlate(core, own, other):
    return correlate_slot(1 - core, other, own, correlate_slot(core, own, own))


def on_device(traces, pair_offsets, pair_counts, pair_owner):
    slot_first, slot_second = pair_blocks(
        pair_offsets, pair_counts, pair_owner, NBLK, SLOT_DEV * NBLK
    )
    seg = lax.axis_index("seg").astype(jnp.int32).reshape(1)
    held = lax.all_to_all(front(traces), "chan", split_axis=0, concat_axis=0, tiled=True)
    sent = select(slot_first, slot_second, seg, held)
    own = lax.all_to_all(sent, ("seg", "chan"), split_axis=0, concat_axis=0, tiled=True)
    other = lax.ppermute(own[:, :64], "seg", [(0, 1), (1, 0), (2, 3), (3, 2)])
    return correlate(seg % 2, own, other)


def solution(mesh):
    placed = (P("chan", "seg", None), P(), P(), P())
    return jax.shard_map(
        on_device,
        mesh=mesh,
        in_specs=placed,
        out_specs=P("seg", "chan", None, None),
        check_vma=False,
    )
```

```python
import math

import jax
import jax.numpy as jnp
import ml_dtypes
import numpy as np
from jax import lax
from jax.experimental import pallas as pl
from jax.experimental.pallas import tpu as pltpu
from jax.sharding import PartitionSpec as P

SAMPLES = 8192
BAND_START = 32
FREQS = 512
HALF = 8
LAGS = 256
BLOCK = 128
NBLK = 32
SEGS = 8
SLOT_DEV = 2
GROUP = 16
RADIX = 16
VMEM = 32 * 1024 * 1024
PAIRS = 2
UNROLL = 32
FETCHES = 8


def bin_order():
    residues = [(0, 8)] + [(unit, RADIX - unit) for unit in range(1, RADIX // 2)]
    return (np.array(residues)[:, :, None] + RADIX * np.arange(FREQS // RADIX)).reshape(-1)


def dft_tables():
    run = SAMPLES // RADIX
    ring = 2.0 * math.pi / SAMPLES * np.arange(SAMPLES)
    bins = bin_order().reshape(RADIX // 2, 1, 2 * FREQS // RADIX)
    phase = np.arange(run)[None, :, None] * (BAND_START + bins) % SAMPLES
    table = np.concatenate([np.cos(ring)[phase], -np.sin(ring)[phase]], axis=2)
    high = table.astype(np.float32).astype(ml_dtypes.bfloat16)
    low = (table - high.astype(np.float64)).astype(np.float32).astype(ml_dtypes.bfloat16)
    return np.concatenate([high, low], axis=2)


def lag_tables():
    shifts = np.arange(LAGS // 2 + 8)
    phase = np.outer(BAND_START + np.arange(FREQS), shifts) % SAMPLES
    angles = phase.astype(np.float32) * np.float32(2.0 * math.pi / SAMPLES)
    norm = 1.0 / math.sqrt(FREQS * SEGS)
    parts = np.stack([np.cos(angles), -np.sin(angles)]).astype(ml_dtypes.bfloat16)
    parts = (parts.astype(np.float32) * norm).astype(ml_dtypes.bfloat16)
    return parts.transpose(0, 2, 1)


def group_mask():
    lane, row = np.arange(256)[None, :], np.arange(GROUP)[:, None]
    return (lane // 16 % 2 * 8 + lane % 8 == row).astype(ml_dtypes.bfloat16)


def pair_blocks(pair_offsets, pair_counts, pair_owner, block_count, slot_count):
    slot_index = lax.iota(jnp.int32, slot_count)
    starts = jnp.cumsum(pair_counts) - pair_counts
    first_block = jnp.sum((starts[None, :] <= slot_index[:, None]).astype(jnp.int32), axis=1) - 1
    member = lax.iota(jnp.int32, block_count)[None, :] == first_block[:, None]
    start_of = jnp.sum(jnp.where(member, starts[None, :], 0), axis=1)
    position = slot_index - start_of
    listed = jnp.sum(jnp.where(member[:, :, None], pair_offsets[None, :, :], 0), axis=1)
    chosen = lax.iota(jnp.int32, pair_offsets.shape[1])[None, :] == position[:, None]
    offset = jnp.sum(jnp.where(chosen, listed, 0), axis=1)
    second_block = jnp.mod(first_block + offset, block_count)
    held = pair_owner[None, :] == slot_index[:, None]
    slot_first = jnp.sum(jnp.where(held, first_block[None, :], 0), axis=1)
    slot_second = jnp.sum(jnp.where(held, second_block[None, :], 0), axis=1)
    return (slot_first, slot_second)


def butterflies(x):
    root, c1, c3 = math.sqrt(0.5), math.cos(math.pi / 8), math.cos(3 * math.pi / 8)
    a = [x[n] + x[n + 8] for n in range(8)]
    b = [x[n] - x[n + 8] for n in range(8)]
    c = [a[n] + a[n + 4] for n in range(4)]
    d = [a[n] - a[n + 4] for n in range(4)]
    even, odd = c[0] + c[2], c[1] + c[3]
    g, h = (d[1] - d[3]) * root, (d[1] + d[3]) * root
    p = [None] + [b[n] - b[8 - n] for n in range(1, 4)]
    q = [None] + [b[n] + b[8 - n] for n in range(1, 4)]
    p2, q2 = p[2] * root, q[2] * root
    re1, re3 = p[1] * c1 + p[3] * c3, p[1] * c3 - p[3] * c1
    im1, im3 = q[1] * c3 + q[3] * c1, q[1] * c1 - q[3] * c3
    plus, minus = b[0] + p2, b[0] - p2
    over, under = q2 + b[4], q2 - b[4]
    return [
        (even + odd, even - odd),
        (plus + re1, im1 + over),
        (d[0] + g, d[2] + h),
        (minus + re3, im3 + under),
        (c[0] - c[2], c[1] - c[3]),
        (minus - re3, im3 - under),
        (d[0] - g, h - d[2]),
        (plus - re1, im1 - over),
    ]


def bin_of(column):
    unit, side, group = column >> 6, (column >> 5) & 1, column & 31
    other = jnp.where(unit == 0, RADIX // 2, RADIX - unit)
    return RADIX * group + jnp.where(side == 0, unit, other)


def front_kernel(
    rows_hbm, dft_hbm, out_ref, rows_ref, dft_ref, band_ref, order_ref, sums_ref, row_sem, table_sem
):
    each = BLOCK * BLOCK // FETCHES
    copies = []
    for fetch in range(FETCHES):
        part = pl.ds(each * fetch, each)
        copies.append(
            pltpu.make_async_copy(rows_hbm.at[part], rows_ref.at[part], row_sem.at[fetch])
        )
        copies[fetch].start()
    table = pltpu.make_async_copy(dft_hbm, dft_ref, table_sem)
    table.start()
    down = lax.broadcasted_iota(jnp.int32, (FREQS, BLOCK), 0)
    across = lax.broadcasted_iota(jnp.int32, (FREQS, BLOCK), 1)
    bins = bin_of(down)
    for tile in range(FREQS // BLOCK):
        lanes = slice(tile * BLOCK, (tile + 1) * BLOCK)
        column = bin_of(across[:8] + tile * BLOCK)[:1]
        near = jnp.abs(bins - column) <= HALF
        band_ref[:, lanes] = jnp.where(near, 1.0, 0.0).astype(jnp.bfloat16)
        order_ref[:, lanes] = jnp.where(down == column, 1.0, 0.0).astype(jnp.bfloat16)

    def channel(chan, carry):
        x = []
        for pair in range(RADIX // 2):
            tile = rows_ref[pl.ds(pl.multiple_of(BLOCK * chan + 16 * pair, 16), 16), :]
            tile = tile.astype(jnp.float32)
            x += [tile[:8], tile[8:]]
        for unit, sums in enumerate(butterflies(x)):
            for side in range(2):
                sums_ref[2 * unit + side, pl.ds(pl.multiple_of(8 * chan, 8), 8), :] = sums[side]
        return carry

    for fetch in range(FETCHES):
        copies[fetch].wait()
        count = BLOCK // FETCHES
        lax.fori_loop(count * fetch, count * (fetch + 1), channel, 0, unroll=4)

    lane = lax.broadcasted_iota(jnp.int32, (1, BLOCK), 1)
    sign = jnp.where((lane < 32) | (lane >= 96), 1.0, -1.0)
    table.wait()
    found = []
    for unit in range(RADIX // 2):
        tiles = []
        for side in range(2):
            for seg in range(2):
                tiles.append(
                    jnp.concatenate(
                        [
                            sums_ref[2 * unit + side, pl.ds(2 * tile + seg, BLOCK, stride=8), :]
                            for tile in range(4)
                        ],
                        axis=1,
                    )
                )
        exact = jnp.concatenate(tiles, axis=0)
        high = exact.astype(jnp.bfloat16)
        low = (exact - high.astype(jnp.float32)).astype(jnp.bfloat16)
        first = jnp.dot(high, dft_ref[unit], preferred_element_type=jnp.float32)
        rest = jnp.dot(low, dft_ref[unit, :, :BLOCK], preferred_element_type=jnp.float32)
        both = first[:, :BLOCK] + (first[:, BLOCK:] + rest)
        one, two = both[: 2 * BLOCK], both[2 * BLOCK :]
        if unit == 0:
            found.append(jnp.where((lane >> 5) & 1 == 0, one, two))
        else:
            found.append(one + sign * pltpu.roll(two, 64, 1))
    left = lax.broadcasted_iota(jnp.int32, (2 * BLOCK, BLOCK), 1) < 64
    real = []
    imag = []
    for one, two in zip(found[0::2], found[1::2]):
        real.append(jnp.where(left, one, pltpu.roll(two, 64, 1)))
        imag.append(jnp.where(left, pltpu.roll(one, 64, 1), two))
    real = jnp.concatenate(real, axis=1)
    imag = jnp.concatenate(imag, axis=1)
    amplitude = jnp.sqrt(real * real + imag * imag)
    high = amplitude.astype(jnp.bfloat16)
    low = (amplitude - high.astype(jnp.float32)).astype(jnp.bfloat16)
    band = band_ref[...]
    total = jnp.dot(high, band, preferred_element_type=jnp.float32)
    total = total + jnp.dot(low, band, preferred_element_type=jnp.float32)
    count = jnp.dot(jnp.ones((8, FREQS), jnp.bfloat16), band, preferred_element_type=jnp.float32)
    divisor = jnp.maximum(total / count[:1], 1.0)
    for part, spectrum in enumerate([real, imag]):
        white = (spectrum / divisor).astype(jnp.bfloat16)
        turned = lax.dot_general(
            order_ref[...], white, (((1,), (1,)), ((), ())), preferred_element_type=jnp.float32
        )
        pieces = [
            turned[:, BLOCK * seg : BLOCK * (seg + 1)].reshape(FREQS // 8, 1, 8, BLOCK)
            for seg in range(2)
        ]
        both = jnp.concatenate(pieces, axis=1).reshape(NBLK, 2 * GROUP, BLOCK)
        out_ref[:, part * 2 * GROUP : (part + 1) * 2 * GROUP, :] = both.astype(jnp.bfloat16)


def select_kernel(first_ref, second_ref, place_ref, held_ref, out_ref, rows_ref):
    lane = lax.broadcasted_iota(jnp.int32, (32, BLOCK), 1)
    left = (lane < 64) == ((place_ref[0] & 1) == 0)

    def turn(block, carry):
        tiles = held_ref[block].astype(jnp.float32)
        rows_ref[block] = jnp.concatenate([tiles, tiles], axis=0).T.astype(jnp.bfloat16)
        return carry

    lax.fori_loop(0, NBLK, turn, 0, unroll=True)

    def send(chan, carry):
        slots = [SLOT_DEV * chan + slot for slot in range(SLOT_DEV)]
        for seg in range(4):
            dest = NBLK * seg + chan
            out_ref[dest, pl.ds(0, 64), :] = held_ref[second_ref[slots[seg % 2]]]
            one = rows_ref[first_ref[slots[0]], pl.ds(32 * seg, 32), :]
            two = rows_ref[first_ref[slots[1]], pl.ds(32 * seg, 32), :]
            out_ref[dest, pl.ds(64, 32), :] = jnp.where(left, one, two)
        return carry

    lax.fori_loop(0, NBLK, send, 0, unroll=True)


def correlate_kernel(
    slot_ref, second_ref, own_ref, mask_ref, table_ref, filled_hbm, out_hbm, cross_ref, lag_ref, out_sem
):
    del filled_hbm
    slot = slot_ref[0]

    def cross(group, carry):
        left = lax.broadcasted_iota(jnp.int32, (32, BLOCK), 1) < 64
        upper = []
        lower = []
        lanes = []
        for seg in range(4):
            src = NBLK * (seg ^ slot) + group
            real, imag = second_ref[src, pl.ds(0, 32), :], second_ref[src, pl.ds(32, 32), :]
            upper += [real, imag]
            lower += [-imag, real]
            lanes.append(own_ref[src, pl.ds(64, 32), :])
        second = jnp.concatenate(
            [jnp.concatenate(upper, axis=0), jnp.concatenate(lower, axis=0)], axis=1
        )
        first = jnp.concatenate(
            [jnp.where(left, lanes[0], lanes[1]), jnp.where(left, lanes[2], lanes[3])], axis=1
        )
        mask = mask_ref[...]
        spread = [jnp.broadcast_to(first[i : i + 1], (GROUP, 256)) * mask for i in range(32)]
        found = jnp.dot(
            jnp.concatenate(spread, axis=0), second, preferred_element_type=jnp.float32
        ).astype(jnp.bfloat16)
        for part in range(2):
            cross_ref[:, NBLK * part + group] = found[:, part * BLOCK : (part + 1) * BLOCK].reshape(
                32, GROUP, BLOCK
            )
        return carry

    def lags(pair, carry):
        sums = []
        for part in range(2):
            tiles = pl.ds(NBLK * part, NBLK)
            sides = [cross_ref[2 * pair + k, tiles].reshape(FREQS, BLOCK) for k in range(2)]
            sums.append(
                jnp.dot(
                    table_ref[part],
                    jnp.concatenate(sides, axis=1),
                    preferred_element_type=jnp.float32,
                )
            )
        later = (sums[0][:BLOCK] + sums[1][:BLOCK]).T
        less = sums[0] - sums[1]
        row = lax.broadcasted_iota(jnp.int32, (8, 2 * BLOCK), 0)
        back = (8 - row) & 7
        turned = []
        for tile in range(15, -1, -1):
            here, above = less[8 * tile : 8 * tile + 8], less[8 * tile + 8 : 8 * tile + 16]
            turned.append(
                jnp.take_along_axis(
                    jnp.where(row == 0, above, here), back, axis=0, mode="promise_in_bounds"
                )
            )
        earlier = jnp.concatenate(turned, axis=0).T
        for k in range(2):
            rows = slice(k * BLOCK, (k + 1) * BLOCK)
            lag_ref[2 * pair + k, :, :BLOCK] = earlier[rows]
            lag_ref[2 * pair + k, :, BLOCK:] = later[rows]
        return carry

    leaving = []
    lax.fori_loop(0, NBLK, cross, 0, unroll=UNROLL)
    for step in range(16 // PAIRS):
        lax.fori_loop(PAIRS * step, PAIRS * (step + 1), lags, 0, unroll=True)
        rows = pl.ds(2 * PAIRS * step, 2 * PAIRS)
        copy = pltpu.make_async_copy(lag_ref.at[rows], out_hbm.at[rows, slot], out_sem.at[step])
        copy.start()
        leaving.append(copy)
    for copy in leaving:
        copy.wait()


def front(traces):
    rows = traces.reshape(BLOCK, 2, SAMPLES // BLOCK, BLOCK).transpose(0, 2, 1, 3)
    rows = rows.reshape(BLOCK * BLOCK, BLOCK)
    return pl.pallas_call(
        front_kernel,
        out_shape=jax.ShapeDtypeStruct((NBLK, 4 * GROUP, BLOCK), jnp.bfloat16),
        in_specs=[pl.BlockSpec(memory_space=pltpu.HBM)] * 2,
        out_specs=pl.BlockSpec(memory_space=pltpu.VMEM),
        scratch_shapes=[
            pltpu.VMEM((BLOCK * BLOCK, BLOCK), jnp.bfloat16),
            pltpu.VMEM((RADIX // 2, SAMPLES // RADIX, 2 * BLOCK), jnp.bfloat16),
            pltpu.VMEM((FREQS, FREQS), jnp.bfloat16),
            pltpu.VMEM((FREQS, FREQS), jnp.bfloat16),
            pltpu.VMEM((RADIX, 8 * BLOCK, BLOCK), jnp.float32),
            pltpu.SemaphoreType.DMA((FETCHES,)),
            pltpu.SemaphoreType.DMA,
        ],
        compiler_params=pltpu.CompilerParams(vmem_limit_bytes=VMEM),
        name="front",
    )(
        pltpu.with_memory_space_constraint(rows, pltpu.HBM),
        pltpu.with_memory_space_constraint(jnp.asarray(dft_tables()), pltpu.HBM),
    )


def select(slot_first, slot_second, place, held):
    smem = pl.BlockSpec(memory_space=pltpu.SMEM)
    return pl.pallas_call(
        select_kernel,
        out_shape=jax.ShapeDtypeStruct((128, 96, BLOCK), jnp.bfloat16),
        in_specs=[smem, smem, smem, pl.BlockSpec(memory_space=pltpu.VMEM)],
        scratch_shapes=[pltpu.VMEM((NBLK, BLOCK, BLOCK), jnp.bfloat16)],
        compiler_params=pltpu.CompilerParams(vmem_limit_bytes=VMEM),
        name="select",
    )(slot_first, slot_second, place, held)


def correlate_slot(slot, second, own, filled=None):
    hbm = pl.BlockSpec(memory_space=pl.ANY)
    vmem = pl.BlockSpec(memory_space=pltpu.VMEM)
    kernel = correlate_kernel
    operands = [slot, second, own, jnp.asarray(group_mask()), jnp.asarray(lag_tables())]
    specs = [pl.BlockSpec(memory_space=pltpu.SMEM)] + [vmem] * 4
    aliases = {}
    if filled is None:
        kernel = lambda *refs: correlate_kernel(*refs[:5], None, *refs[5:])
    else:
        operands.append(filled)
        specs.append(hbm)
        aliases = {5: 0}
    return pl.pallas_call(
        kernel,
        out_shape=jax.ShapeDtypeStruct((32, SLOT_DEV, BLOCK, LAGS), jnp.float32),
        in_specs=specs,
        out_specs=hbm,
        scratch_shapes=[
            pltpu.VMEM((32, 2 * NBLK, GROUP, BLOCK), jnp.bfloat16),
            pltpu.VMEM((32, BLOCK, LAGS), jnp.float32),
            pltpu.SemaphoreType.DMA((16 // PAIRS,)),
        ],
        input_output_aliases=aliases,
        compiler_params=pltpu.CompilerParams(vmem_limit_bytes=24 * 1024 * 1024),
        cost_estimate=pl.CostEstimate(flops=8 << 30, transcendentals=0, bytes_accessed=9 << 20),
        name="correlate_first" if filled is None else "correlate_second",
    )(*operands)


def correlate(core, own, other):
    return correlate_slot(1 - core, other, own, correlate_slot(core, own, own))


def on_device(traces, pair_offsets, pair_counts, pair_owner):
    slot_first, slot_second = pair_blocks(
        pair_offsets, pair_counts, pair_owner, NBLK, SLOT_DEV * NBLK
    )
    seg = lax.axis_index("seg").astype(jnp.int32).reshape(1)
    held = lax.all_to_all(front(traces), "chan", split_axis=0, concat_axis=0, tiled=True)
    sent = select(slot_first, slot_second, seg, held)
    own = lax.all_to_all(sent, ("seg", "chan"), split_axis=0, concat_axis=0, tiled=True)
    other = lax.ppermute(own[:, :64], "seg", [(0, 1), (1, 0), (2, 3), (3, 2)])
    return correlate(seg % 2, own, other)


def solution(mesh):
    placed = (P("chan", "seg", None), P(), P(), P())
    return jax.shard_map(
        on_device,
        mesh=mesh,
        in_specs=placed,
        out_specs=P("seg", "chan", None, None),
        check_vma=False,
    )
```
